32 devices in a mesh: leaf: 8 (over z, y), row: 4 (over x, core).
Axes of the slice: x: 2, y: 2, z: 4, core: 2. Of those that a mesh axis runs over, the one named last changes fastest.
Arguments:
- panel0: float32 [12288, 512], P(('leaf', 'row')), may hold values from -3 to 30, as said below
- panel1: float32 [6144, 512], P(('leaf', 'row')), may hold values from -3 to 30
- panel2: float32 [3072, 512], P(('leaf', 'row')), may hold values from -3 to 30
- panel3: float32 [1536, 512], P(('leaf', 'row')), may hold values from -3 to 30
- maps1: int32 [8, 8], replicated, may hold values from 0 to 11, as said below
- maps2: int32 [4, 8], replicated, may hold values from 0 to 11, as said below
- maps3: int32 [2, 8], replicated, may hold values from 0 to 11, as said below
Outputs:
- update_top: float32 [1024, 1024], P(('leaf', 'row'))
The draws below stay inside these ranges and needn't reach their ends.
Inputs may be any that keep to these rules, and one draw needn't show every extreme that they name: `panel0`: each front's first 512 rows form a symmetric matrix, and every assembled pivot block is positive definite. `maps1`: each row lists distinct parent block numbers. `maps2`: each row lists distinct parent block numbers. `maps3`: each row lists distinct parent block numbers.
All inputs are finite; a program needn't handle non-finite values.
Results may differ from the reference program's by a relative error of at most 0.0003.
Values sent between devices are 32-bit elements; how exact they have to be, the bound alone decides.
A program may use at most 128 MiB of HBM per device.

```python
import math
import jax
import jax.numpy as jnp
from jax import lax

BLOCK = 128
PIV = 512
UPD = 1024
N_LEAF = 8


def draw_noise(key, shape):
    return jnp.clip(jax.random.normal(key, shape, jnp.float32), -4.0, 4.0)


def make_panels(key, front_count):
    keys = jax.random.split(key, 3)
    diagonal = jax.random.uniform(keys[0], (front_count, PIV), jnp.float32, 12.0, 24.0)
    raw = draw_noise(keys[1], (front_count, PIV, PIV)) * (3.6 / math.sqrt(PIV))
    pivot = (raw + jnp.swapaxes(raw, 1, 2)) / math.sqrt(2.0)
    pivot = pivot + diagonal[:, :, None] * jnp.eye(PIV, dtype=jnp.float32)[None, :, :]
    coupling = draw_noise(keys[2], (front_count, UPD, PIV)) * (3.0 / math.sqrt(PIV))
    stacked = jnp.concatenate([pivot, coupling], axis=1)
    return stacked.reshape(front_count * (PIV + UPD), PIV)


def make_maps(key, child_count):
    keys = jax.random.split(key, child_count)
    parent_blocks = (PIV + UPD) // BLOCK

    def one_row(one_key):
        return jax.random.permutation(one_key, parent_blocks)[:UPD // BLOCK]
    return jax.vmap(one_row)(keys).astype(jnp.int32)


def draw_panel0(key, part):
    return make_panels(jax.random.fold_in(key, 10), N_LEAF)


def draw_panel1(key, part):
    return make_panels(jax.random.fold_in(key, 11), N_LEAF // 2)


def draw_panel2(key, part):
    return make_panels(jax.random.fold_in(key, 12), N_LEAF // 4)


def draw_panel3(key, part):
    return make_panels(jax.random.fold_in(key, 13), N_LEAF // 8)


def draw_maps1(key, part):
    return make_maps(jax.random.fold_in(key, 21), N_LEAF)


def draw_maps2(key, part):
    return make_maps(jax.random.fold_in(key, 22), N_LEAF // 2)


def draw_maps3(key, part):
    return make_maps(jax.random.fold_in(key, 23), N_LEAF // 4)


def setup_inputs(seed: int = 0) -> dict:
    splits = jax.random.split(jax.random.key(seed), 8)
    panel0 = draw_panel0(jax.random.fold_in(splits[7], 71), 0)
    panel1 = draw_panel1(jax.random.fold_in(splits[7], 71), 0)
    panel2 = draw_panel2(jax.random.fold_in(splits[7], 71), 0)
    panel3 = draw_panel3(jax.random.fold_in(splits[7], 71), 0)
    maps1 = draw_maps1(jax.random.fold_in(splits[7], 71), 0)
    maps2 = draw_maps2(jax.random.fold_in(splits[7], 71), 0)
    maps3 = draw_maps3(jax.random.fold_in(splits[7], 71), 0)
    return {"panel0": panel0, "panel1": panel1, "panel2": panel2, "panel3": panel3, "maps1": maps1, "maps2": maps2, "maps3": maps3}


exact_mode = lax.Precision.HIGHEST

def extend_add(update, blocks):
    parent_blocks = (PIV + UPD) // BLOCK
    child_blocks = blocks.shape[0]
    onehot = (blocks[:, None] == jnp.arange(parent_blocks, dtype=jnp.int32)[None, :]).astype(jnp.float32)
    tile_grid = update.reshape(child_blocks, BLOCK, child_blocks, BLOCK)
    spread = jnp.einsum('ia,ixjy->axjy', onehot, tile_grid, precision=exact_mode)
    placed = jnp.einsum('axjy,jb->axby', spread, onehot, precision=exact_mode)
    return placed.reshape(parent_blocks * BLOCK, parent_blocks * BLOCK)

def factor_front(front_rows, trailing, upper_panel):
    assembled = front_rows + upper_panel
    factor = jnp.linalg.cholesky(assembled[:PIV])
    columns = lax.linalg.triangular_solve(factor, assembled[PIV:], left_side=False, lower=True, transpose_a=True)
    return trailing - jnp.dot(columns.astype(jnp.float32), columns.T.astype(jnp.float32), precision=exact_mode, preferred_element_type=jnp.float32)

def reference(panel0, panel1, panel2, panel3, maps1, maps2, maps3):
    front_size = PIV + UPD
    child_blocks = UPD // BLOCK
    fronts = panel0.reshape(N_LEAF, front_size, PIV)

    def leaf_front(front_rows):
        return factor_front(front_rows, jnp.zeros((UPD, UPD), jnp.float32), jnp.zeros((front_size, PIV), jnp.float32))
    schur = lax.map(leaf_front, fronts)
    level_index = 1
    for panel_rows, block_maps in ((panel1, maps1), (panel2, maps2), (panel3, maps3)):
        front_count = N_LEAF // 2 ** level_index
        fronts = panel_rows.reshape(front_count, front_size, PIV)
        children = schur.reshape(front_count, 2, UPD, UPD)
        map_pairs = block_maps.reshape(front_count, 2, child_blocks)

        def parent(inputs):
            front_rows, child_pair, map_pair = inputs
            upper = extend_add(child_pair[0], map_pair[0]) + extend_add(child_pair[1], map_pair[1])
            return factor_front(front_rows, upper[PIV:, PIV:], upper[:, :PIV])
        schur = lax.map(parent, (fronts, children, map_pairs))
        level_index = level_index + 1
    return schur.reshape(N_LEAF // 8 * UPD, UPD)
```

```python
import functools
import math

import jax
import jax.numpy as jnp
from jax import lax
from jax.experimental import pallas as pl
from jax.experimental.pallas import tpu as pltpu
from jax.sharding import PartitionSpec as P

BLOCK = 128
SUB = 8
LEVELS = 4
CONTRACT_LAST = (((1,), (1,)), ((), ()))
CONTRACT_FIRST = (((1,), (0,)), ((), ()))


def halves(value):
    high = value.astype(jnp.bfloat16)
    low = (value - high.astype(jnp.float32)).astype(jnp.bfloat16)
    return high, low


def dot_split(left, right):
    left_high, left_low = left
    right_high, right_low = right

    def one(a, b):
        return lax.dot_general(a, b, CONTRACT_LAST, preferred_element_type=jnp.float32)

    return one(left_high, right_high) + (one(left_high, right_low) + one(left_low, right_high))


def dot_nt(left, right):
    return dot_split(halves(left), halves(right))


def spread(value, rows, columns):
    return jnp.broadcast_to(value, (rows, columns))


def diagonal_inverse(block, pause):
    count = BLOCK // SUB
    rows = [block[v * SUB : (v + 1) * SUB] for v in range(count)]
    lane = lax.broadcasted_iota(jnp.int32, (SUB, BLOCK), 1)
    sub = lax.broadcasted_iota(jnp.int32, (SUB, BLOCK), 0)
    for b in range(count):
        if b == count // 2:
            pause()
        base = b * SUB
        inside = (lane >= base) & (lane < base + SUB)
        own = rows[b]
        columns = [spread(own[:, base + j : base + j + 1], SUB, BLOCK) for j in range(SUB)]
        a = [
            [spread(columns[j][i : i + 1], SUB, BLOCK) for j in range(i + 1)] for i in range(SUB)
        ]
        inverse = []
        ratio = [[None] * SUB for _ in range(SUB)]
        for i in range(SUB):
            inverse.append(1.0 / a[i][i])
            for j in range(i + 1, SUB):
                ratio[j][i] = a[j][i] * inverse[i]
            for j in range(i + 1, SUB):
                for k in range(i + 1, j + 1):
                    a[j][k] = a[j][k] - ratio[j][i] * a[k][i]
        cleared = jnp.where(inside, 0.0, own)
        pivots = []
        for j in range(SUB):
            row = spread(cleared[j : j + 1], SUB, BLOCK)
            row = jnp.where(lane == base + j, 1.0, row)
            for i in range(j):
                row = row - ratio[j][i] * pivots[i]
            pivots.append(row)
        for v in range(b + 1, count):
            old = rows[v]
            new = jnp.where(inside, 0.0, old)
            factors = []
            for j in range(SUB):
                column = spread(old[:, base + j : base + j + 1], SUB, BLOCK)
                for i in range(j):
                    column = column - factors[i] * a[j][i]
                factors.append(column * inverse[j])
            for j in range(SUB):
                new = new - factors[j] * pivots[j]
            rows[v] = new
        final = jnp.zeros((SUB, BLOCK), jnp.float32)
        scale = jnp.ones((SUB, BLOCK), jnp.float32)
        for j in range(SUB):
            final = jnp.where(sub == j, pivots[j], final)
            scale = jnp.where(sub == j, a[j][j], scale)
        rows[b] = jnp.where(lane <= sub + base, final / jnp.sqrt(scale), 0.0)
    return jnp.concatenate(rows, axis=0)


def neighbours(level):
    leaf = lax.axis_index("leaf")
    row = lax.axis_index("row")
    partners = []
    for bit in range(level):
        flag = leaf // 2**bit % 2
        partners.append({"leaf": leaf + (1 - 2 * flag) * 2**bit, "row": row})
    count = lax.axis_size("row")
    sibling = row + 1 - 2 * (row % 2)
    forward = [lax.rem(row + 2 * d, count) for d in range(1, count // 2)]
    backward = [lax.rem(row + count - 2 * d, count) for d in range(1, count // 2)]
    across = [{"leaf": leaf, "row": other} for other in forward]
    return partners, {"leaf": leaf, "row": sibling}, across, backward


def remote(source, target, sends, receives, slot, device):
    return pltpu.make_async_remote_copy(
        src_ref=source,
        dst_ref=target,
        send_sem=sends.at[slot],
        recv_sem=receives.at[slot],
        device_id=device,
        device_id_type=pl.DeviceIdType.MESH,
    )


class Gather:
    def __init__(self, buffer, place, sends, receives, slot, near, source=None):
        _, sibling, across, origins = near
        own = buffer.at[place(lax.axis_index("row"))]
        if source is None:
            source = own
        self.direct = remote(source, own, sends, receives, slot, sibling)
        self.far = []
        self.relay = []
        for n, (device, origin) in enumerate(zip(across, origins)):
            self.far.append(remote(source, own, sends, receives, slot + 1 + 2 * n, device))
            passed = buffer.at[place(origin)]
            self.relay.append(remote(passed, passed, sends, receives, slot + 2 + 2 * n, sibling))

    def start(self):
        for copy in self.far:
            copy.start()
        self.direct.start()

    def pass_on(self):
        for copy, relay in zip(self.far, self.relay):
            copy.wait_recv()
            relay.start()

    def finish(self):
        self.direct.wait_recv()
        for relay in self.relay:
            relay.wait_recv()
        for copy in [self.direct] + self.far + self.relay:
            copy.wait_send()


def rows_at(size, base=0):
    def place(row):
        return pl.ds(pl.multiple_of(row * size + base, 8), size)

    return place


def column_tiles(order):
    count = order // BLOCK
    return [(i, j) for j in range(count) for i in range(j, count)]


def pivot_chunks(order):
    count = order // BLOCK
    return [(0, 1), (1, count), (count, 2 * count - 1), (2 * count - 1, len(column_tiles(order)))]


def dot_split_nn(left, right):
    left_high, left_low = left
    right_high, right_low = right

    def one(a, b):
        return lax.dot_general(a, b, CONTRACT_FIRST, preferred_element_type=jnp.float32)

    return one(left_high, right_high) + (one(left_high, right_low) + one(left_low, right_high))


def entry_barrier(near):
    partners, sibling, across, _ = near
    barrier = pltpu.get_barrier_semaphore()
    peers = partners + [sibling] + across
    for peer in peers:
        pl.semaphore_signal(barrier, inc=1, device_id=peer, device_id_type=pl.DeviceIdType.MESH)
    pl.semaphore_wait(barrier, len(peers))


def bit_reversed(index, bits):
    return sum((index >> b & 1) << (bits - 1 - b) for b in range(bits))


def rows_at_scaled(stride, base, size):
    def place(row):
        return pl.ds(pl.multiple_of(row * stride + base, 8), size)

    return place


class Links:
    def __init__(self, near, sends, receives):
        self.near = near
        self.sends = sends
        self.receives = receives
        self.used = 0

    def copy(self, source, target, device):
        slot = self.used
        self.used += 1
        return remote(source, target, self.sends, self.receives, slot, device)

    def gather(self, buffer, place, source=None):
        slot = self.used
        self.used += 1 + 2 * len(self.near[2])
        return Gather(buffer, place, self.sends, self.receives, slot, self.near, source)


def gather_task(move):
    return [move.start, move.pass_on, move.finish]


def sum_task(links, bits, share, start, height, inbox, sums, target, stride, base):
    row = lax.axis_index("row")
    partners = links.near[0]
    span = pl.ds(start, height)
    place = rows_at_scaled(stride, base, height)
    moves = []
    for k, bit in enumerate(bits):
        source = share.at[span] if k == 0 else sums.at[k - 1, span]
        moves.append(links.copy(source, inbox.at[k, span], partners[bit]))
    spread = links.gather(target, place)

    def advance(k):
        moves[k].wait()
        total = (share[span] if k == 0 else sums[k - 1, span]) + inbox[k, span]
        if k + 1 < len(bits):
            sums[k, span] = total
            moves[k + 1].start()
        else:
            target[place(row)] = total
            spread.start()

    steps = [functools.partial(advance, k) for k in range(len(bits))]
    return [moves[0].start] + steps + [spread.pass_on, spread.finish]


def scatter_task(links, bits, share, start, height, inbox, sums, target, stride):
    row = lax.axis_index("row")
    leaf = lax.axis_index("leaf")
    partners = links.near[0]
    flags = [leaf // 2**bit % 2 for bit in bits]
    heights = [height // 2 ** (k + 1) for k in range(len(bits))]
    moves = []
    for k, bit in enumerate(bits):
        size = heights[k]
        other = pl.multiple_of((1 - flags[k]) * size, 8)
        if k == 0:
            source = share.at[pl.ds(start + other, size)]
        else:
            source = sums.at[k - 1, pl.ds(other, size)]
        moves.append(links.copy(source, inbox.at[k, pl.ds(0, size)], partners[bit]))
    regions = []
    origin = row * stride + start
    for flag, size in zip(flags, heights):
        origin = origin + flag * size
        regions.append(pl.ds(pl.multiple_of(origin, 8), size))
    returns = []
    for region, bit in reversed(list(zip(regions, bits))):
        returns.append(links.copy(target.at[region], target.at[region], partners[bit]))
    spread = links.gather(target, rows_at_scaled(stride, start, height))

    def reduce(k):
        size = heights[k]
        moves[k].wait()
        keep = pl.multiple_of(flags[k] * size, 8)
        mine = share[pl.ds(start + keep, size)] if k == 0 else sums[k - 1, pl.ds(keep, size)]
        total = mine + inbox[k, :size]
        if k + 1 < len(bits):
            sums[k, :size] = total
            moves[k + 1].start()
        else:
            target[regions[-1]] = total
            returns[0].start()

    def widen(k):
        returns[k].wait()
        if k + 1 < len(bits):
            returns[k + 1].start()
        else:
            spread.start()

    down = [functools.partial(reduce, k) for k in range(len(bits))]
    up = [functools.partial(widen, k) for k in range(len(bits))]
    return [moves[0].start] + down + up + [spread.pass_on, spread.finish]


def extra_task(links, bits, extra, columns, inbox, middle, final_in, result):
    leaf = lax.axis_index("leaf")
    partners = links.near[0]
    flags = [leaf // 2**bit % 2 for bit in range(LEVELS - 1)]
    size = result.shape[0]
    near, far = bits[0], bits[1]

    def pick(axis, flag):
        return (pl.ds(flag, 1), pl.ds(0, 2)) if axis == 0 else (pl.ds(0, 2), pl.ds(flag, 1))

    def inner(flag):
        return (pl.ds(0, 1), pl.ds(flag, 1)) if near == 0 else (pl.ds(flag, 1), pl.ds(0, 1))

    deep = LEVELS - 2
    half = lambda flag: pl.ds(pl.multiple_of(flag * size, 8), size)
    whole = pl.ds(0, 2 * size)
    give = extra.at[(*pick(near, 1 - flags[near]), whole, columns)]
    moves = [links.copy(give, inbox, partners[near])]
    moves.append(links.copy(middle.at[0].at[inner(1 - flags[far])], middle.at[1].at[(pl.ds(0, 1), pl.ds(0, 1))], partners[far]))
    moves.append(links.copy(final_in.at[0, half(1 - flags[deep])], final_in.at[1, pl.ds(0, size)], partners[deep]))

    def one():
        moves[0].wait()
        middle[0] = extra[(*pick(near, flags[near]), whole, columns)] + inbox[...]
        moves[1].start()

    def two():
        moves[1].wait()
        kept = middle[(0, *inner(flags[far]))] + middle[1, :1, :1]
        final_in[0] = kept.reshape(kept.shape[2:])
        moves[2].start()

    def three():
        moves[2].wait()
        result[...] = final_in[0, half(flags[deep])] + final_in[1, :size]

    return [moves[0].start, one, two, three]


def factor(diagonal, column, lower, inverse, spare, hook):
    order = lower.shape[1]
    tiles = order // BLOCK
    product, cross, block = spare
    row_ids = lax.broadcasted_iota(jnp.int32, (order, BLOCK), 0)

    def store(target, where, value):
        high, low = halves(value)
        target[(0, *where)] = high
        target[(1, *where)] = low

    def step(j, carry):
        hook(j, 0)
        start = pl.multiple_of(j * BLOCK, BLOCK)
        span = pl.ds(start, BLOCK)
        mine = lower[0, span], lower[1, span]
        product[...] = dot_split((lower[0], lower[1]), mine)
        cross[...] = dot_split_nn(mine, (inverse[0], inverse[1]))
        block[...] = diagonal_inverse(
            diagonal(j) - dot_split(mine, mine), functools.partial(hook, j, 1)
        )
        hook(j, 2)
        own = halves(block[...])
        below = jnp.where(row_ids >= start + BLOCK, column(j) - product[...], 0.0)
        store(lower, (slice(None), span), dot_split(halves(below), own))
        store(inverse, (span, slice(None)), -dot_split_nn(own, halves(cross[...])))
        inverse[0, span, span] = own[0]
        inverse[1, span, span] = own[1]
        return carry

    lax.fori_loop(0, tiles, step, 0)


def front_kernel(level, row_count, front, order, *refs):
    last = level == LEVELS - 1
    first = level == 0
    group = 2**level
    below = front - order
    refs = list(refs)
    take = lambda: refs.pop(0)
    row = lax.axis_index("row")
    member = lax.axis_index("leaf") % group
    panels = joined = ()
    if first:
        panel, *panels = take(), take()
    else:
        pivot_share, below_share = take(), take()
    if level == 1:
        panels = [take() for _ in range(LEVELS - 2)]
    if last:
        extra = take()
    result = take()
    joined = [take() for _ in panels]
    lower, inverse, product, cross, block, columns, sends, receives = [take() for _ in range(8)]
    held = [take() for _ in panels]
    near = neighbours(level)
    links = Links(near, sends, receives)
    lower[...] = jnp.zeros_like(lower)
    inverse[...] = jnp.zeros_like(inverse)
    entry_barrier(near)
    panel_tasks = []
    for part, buffer in zip(panels, held):
        size = part.shape[0]
        panel_tasks.append(gather_task(links.gather(buffer, rows_at(size), part)))
        buffer[rows_at(size)(row)] = part[...]
    if first:
        gathered = take()
        chunk = panel.shape[0]

        def piece(base, size, left, width):
            def place(index):
                return rows_at_scaled(chunk, base, size)(index), pl.ds(left, width)

            source = panel.at[pl.ds(base, size), pl.ds(left, width)]
            return gather_task(links.gather(gathered, place, source))

        step = math.gcd(chunk, BLOCK)
        strips = [piece(base, step, 0, BLOCK) for base in range(0, chunk, step)]
        strips += [piece(0, chunk, left, BLOCK) for left in range(BLOCK, order, BLOCK)]
        for strip in strips:
            strip[0]()
        own = pl.ds(pl.multiple_of(row * chunk, 8), chunk)
        gathered[own] = panel[...]
        panel_tasks[0][0]()
        lead = chunk // step
        early = BLOCK // step
        for stage in (1, 2):
            for strip in strips[:early]:
                strip[stage]()
        rest = strips[early:lead]
        plan = {(0, 1): [s[1] for s in rest], (0, 2): [s[2] for s in rest]}
        for n, strip in enumerate(strips[lead:]):
            plan[n, 2] = plan.get((n, 2), []) + [strip[1]]
            plan[n + 1, 0] = [strip[2]]
        after = panel_tasks[0][1:]

        def diagonal(j):
            span = pl.ds(pl.multiple_of(j * BLOCK, BLOCK), BLOCK)
            return gathered[span, span]

        def column(j):
            return gathered[:order, pl.ds(pl.multiple_of(j * BLOCK, BLOCK), BLOCK)]

    else:
        packed, pivot_sum, pivot_in, below_sum, below_in = [take() for _ in range(5)]
        tasks = []
        turns = [list(range(level)), list(range(level))]
        if level > 1:
            turns[1][0], turns[1][1] = 1, 0
        for n, (begin, end) in enumerate(pivot_chunks(order)):
            size = BLOCK // row_count
            height = (end - begin) * size
            bits = turns[n % 2] if n else turns[0]
            tasks.append(
                sum_task(
                    links, bits, pivot_share, begin * size, height, pivot_in, pivot_sum,
                    packed, height, begin * BLOCK,
                )
            )
        share = below_share.shape[0]
        for n in range(2):
            height = share // 2
            if last:
                tasks.append(
                    scatter_task(
                        links, turns[n], below_share, n * height, height, below_in.at[n],
                        below_sum.at[n], columns, share,
                    )
                )
            else:
                tasks.append(
                    sum_task(
                        links, turns[n], below_share, n * height, height, below_in, below_sum,
                        columns, share, n * height,
                    )
                )
        a, b, c, d, e, f = tasks
        both = lambda k: [e[k], f[k]]
        pre = [t[0] for t in tasks]
        if level == 1:
            pre += [a[1], b[1], a[2], c[1], d[1]] + [t[0] for t in panel_tasks] + [b[2], a[3]]
            plan = {
                (0, 1): [c[2], d[2]],
                (0, 2): [b[3]],
                (1, 0): [c[3], e[1]],
                (1, 1): [d[3]],
                (2, 1): [f[1]] + [t[1] for t in panel_tasks],
                (3, 0): [e[2]],
                (3, 1): [e[3]] + [t[2] for t in panel_tasks],
            }
            after = [f[2], f[3]]
        elif level == 2:
            pre += [a[1], b[1], c[1], d[1], a[2], b[2], c[2], d[2], a[3], b[3], a[4]]
            plan = {
                (0, 1): [c[3], d[3]] + both(1),
                (0, 2): [b[4]],
                (1, 0): [c[4]],
                (1, 1): [d[4]],
                (2, 0): both(2),
                (3, 1): [e[3]],
                (3, 2): [e[4]],
            }
            after = [f[3], f[4]]
        else:
            inbox0, middle0, final0, inbox1, middle1, final1, sums0, sums1 = [take() for _ in range(8)]
            half = below // 2
            x = extra_task(links, (0, 1), extra, pl.ds(0, half), inbox0, middle0, final0, sums0)
            y = extra_task(links, (1, 0), extra, pl.ds(half, half), inbox1, middle1, final1, sums1)
            pre += [a[1], b[1], c[1], d[1], a[2], b[2], c[2], d[2]] + both(1) + [x[0], y[0]]
            pre += [a[3], b[3], a[4], c[3], d[3], b[4], a[5]]
            plan = {
                (0, 1): both(2) + [c[4], d[4]],
                (0, 2): [b[5]],
                (1, 0): [c[5]] + both(3),
                (1, 1): [x[1], y[1]] + both(4),
                (2, 0): [d[5]] + both(5),
                (2, 1): [x[2], y[2]],
                (2, 2): both(6),
                (3, 1): [x[3], y[3]],
                (3, 2): [e[7]],
            }
            after = [f[7], e[8], f[8]]
        for action in pre:
            action()

        count = order // BLOCK

        def diagonal(j):
            place = j * count - j * (j - 1) // 2
            return packed[pl.ds(pl.multiple_of(place * BLOCK, BLOCK), BLOCK)]

        def column(j):
            place = j * count - j * (j - 1) // 2 - j
            return packed[pl.ds(pl.multiple_of(place * BLOCK, BLOCK), order)]

    def hook(j, slot):
        for (when, which), actions in plan.items():
            if which == slot:

                @pl.when(j == when)
                def _():
                    for action in actions:
                        action()

    factor(diagonal, column, lower, inverse, (product, cross, block), hook)
    for action in after:
        action()
    if last:
        height = result.shape[0]
        position = member * row_count + row
        own = columns[pl.ds(pl.multiple_of(position * height, 8), height)]
        whole = inverse[0], inverse[1]
        weight = dot_split_nn(halves(dot_split(halves(own), whole)), whole)
        rest = dot_nt(weight, columns[...])
        result[:, :half] = sums0[...] - rest[:, :half]
        result[:, half:] = sums1[...] - rest[:, half:]
        return
    width = order // group
    if first:
        for left in range(0, order, 2 * BLOCK):
            right = min(left + 2 * BLOCK, order)
            part = inverse[0, left:right, :right], inverse[1, left:right, :right]
            result[:, left:right] = dot_split(halves(gathered[order:, :right]), part)
    else:
        span = pl.ds(pl.multiple_of(member * width, BLOCK), width)
        result[...] = dot_split(halves(columns[...]), (inverse[0, span], inverse[1, span]))
    for buffer, target in zip(held, joined):
        target[...] = buffer[...]


def share_kernel(level, row_count, front, order, *refs):
    group = 2**level
    below = front - order
    refs = list(refs)
    take = lambda: refs.pop(0)
    inverse_map, next_panel, fresh = take(), take(), take()
    old = take() if level else None
    kept, pivot_out, below_out = take(), take(), take()
    extra = take() if level == LEVELS - 2 else None
    placed, whole_panel, everything = take(), take(), take()
    row = lax.axis_index("row")
    depth = 0 if old is None else old.shape[1]
    width = order // group
    if old is not None:
        kept[:below, :depth] = old[:below]
    kept[:below, depth:] = fresh[...]
    kept[below:] = jnp.zeros((BLOCK, depth + width), jnp.float32)
    for i in range(front // BLOCK):
        block = pl.multiple_of(inverse_map[i] * BLOCK, BLOCK)
        placed[i * BLOCK : (i + 1) * BLOCK] = kept[pl.ds(block, BLOCK)]
    held = next_panel.shape[0]
    whole_panel[...] = jnp.zeros_like(whole_panel)
    place = lax.axis_index("leaf") % (2 * group)
    whole_panel[pl.ds(pl.multiple_of(place * held, 8), held)] = next_panel[...]
    pivots = halves(placed[:order])
    for t, (i, j) in enumerate(column_tiles(order)):
        down = slice(i * BLOCK, (i + 1) * BLOCK)
        along = slice(j * BLOCK, (j + 1) * BLOCK)
        product = dot_split([p[down] for p in pivots], [p[along] for p in pivots])
        everything[t * BLOCK : (t + 1) * BLOCK] = whole_panel[down, along] - product
    for begin, end in pivot_chunks(order):
        size = BLOCK // row_count
        height = (end - begin) * size
        mine = rows_at_scaled(height, begin * BLOCK, height)(row)
        pivot_out[begin * size : end * size] = everything[mine]
    height = below_out.shape[0]
    mine = rows_at_scaled(height, order, height)(row)
    below_out[...] = whole_panel[mine] - dot_split(halves(placed[mine]), pivots)
    kept[:below] = placed[order:]
    if level == LEVELS - 2:
        top = 2 * group
        height = below // (top * row_count)
        for index in range(top):
            start = pl.multiple_of(order + (index * row_count + row) * height, 8)
            spot = bit_reversed(index, LEVELS - 1)
            placed[spot * height : (spot + 1) * height] = placed[pl.ds(start, height)]
        own_part = halves(placed[: top * height])
        value = -dot_split(own_part, halves(kept[:below]))
        extra[...] = value.reshape(extra.shape)


def front_step(level, row_count, front, order, operands):
    below = front - order
    width = order // 2**level
    share = len(column_tiles(order)) * BLOCK // row_count
    float32 = jnp.float32

    def vmem(*shape, dtype=float32):
        return pltpu.VMEM(shape, dtype)

    def out(*shape):
        return jax.ShapeDtypeStruct(shape, float32)

    last = level == LEVELS - 1
    rest = below // row_count
    top = 2 ** (LEVELS - 1)
    copies = 8 * (row_count - 1) + 32
    scratch = [
        vmem(2, order, order, dtype=jnp.bfloat16),
        vmem(2, order, order, dtype=jnp.bfloat16),
        vmem(order, BLOCK),
        vmem(BLOCK, order),
        vmem(BLOCK, BLOCK),
        vmem(below if level else 8, order),
        pltpu.SemaphoreType.DMA((copies,)),
        pltpu.SemaphoreType.DMA((copies,)),
    ]
    panels = operands[1:] if level == 0 else operands[2:] if level == 1 else []
    heights = [row_count * panel.shape[0] for panel in panels]
    scratch += [vmem(height, order) for height in heights]
    if level == 0:
        scratch.append(vmem(front, order))
    else:
        scratch += [
            vmem(share * row_count, BLOCK),
            vmem(level, share, BLOCK),
            vmem(level, share, BLOCK),
        ]
        if last:
            scratch += [vmem(2, level, rest // 4, order), vmem(2, level, rest // 4, order)]
        else:
            scratch += [vmem(level, rest, order), vmem(level, rest, order)]
    if last:
        height = rest // top
        half = below // 2
        for shape in ((1, 2), (2, 1)):
            scratch += [
                vmem(*shape, 2 * height, half),
                vmem(2, *shape, 2 * height, half),
                vmem(2, 2 * height, half),
            ]
        scratch += [vmem(height, half), vmem(height, half)]
        shapes = out(height, below)
    else:
        shapes = [out(below, width)] + [out(height, order) for height in heights]
    specs = [pl.BlockSpec(memory_space=pltpu.VMEM)] * len(operands)
    return pl.pallas_call(
        functools.partial(front_kernel, level, row_count, front, order),
        out_shape=shapes,
        in_specs=specs,
        scratch_shapes=scratch,
        name=f"front{level}",
        compiler_params=pltpu.CompilerParams(
            vmem_limit_bytes=60 * 2**20, collective_id=level, has_side_effects=True
        ),
    )(*operands)


def share_step(level, row_count, front, order, operands):
    below = front - order
    depth = sum(order // 2**k for k in range(level + 1))
    tiles = len(column_tiles(order))
    rest = below // row_count

    def out(*shape):
        return jax.ShapeDtypeStruct(shape, jnp.float32)

    shapes = [out(below + BLOCK, depth), out(tiles * BLOCK // row_count, BLOCK), out(rest, order)]
    if level == LEVELS - 2:
        shapes.append(out(2, 2, rest // 4, below))
    specs = [pl.BlockSpec(memory_space=pltpu.VMEM)] * len(operands)
    specs[0] = pl.BlockSpec(memory_space=pltpu.SMEM)
    return pl.pallas_call(
        functools.partial(share_kernel, level, row_count, front, order),
        out_shape=shapes,
        in_specs=specs,
        scratch_shapes=[
            pltpu.VMEM((front, depth), jnp.float32),
            pltpu.VMEM((front, order), jnp.float32),
            pltpu.VMEM((tiles * BLOCK, BLOCK), jnp.float32),
        ],
        name=f"share{level}",
        compiler_params=pltpu.CompilerParams(vmem_limit_bytes=60 * 2**20),
    )(*operands)


def body(panel0, panel1, panel2, panel3, maps1, maps2, maps3):
    block_maps = (maps1, maps2, maps3)
    row_count = lax.axis_size("row")
    leaf = lax.axis_index("leaf")
    order = panel0.shape[1]
    front = panel0.shape[0] * row_count
    parents = front // BLOCK
    children = (front - order) // BLOCK
    operands = [panel0, panel1]
    waiting = [[], [panel2, panel3], []]
    old = []
    panels = []
    for level in range(LEVELS - 1):
        blocks = lax.dynamic_index_in_dim(block_maps[level], leaf // 2**level, 0, keepdims=False)
        hit = blocks[None, :] == jnp.arange(parents, dtype=jnp.int32)[:, None]
        back = jnp.min(
            jnp.where(hit, jnp.arange(children, dtype=jnp.int32)[None, :], children), axis=1
        )
        fresh, *joined = front_step(level, row_count, front, order, operands + waiting[level])
        panels += joined
        shared = [back, panels[level], fresh] + old
        outs = share_step(level, row_count, front, order, shared)
        old = [outs[0]]
        operands = list(outs[1:])
    return front_step(LEVELS - 1, row_count, front, order, operands)


def solution(mesh):
    rows = P(("leaf", "row"), None)
    return jax.shard_map(
        body,
        mesh=mesh,
        in_specs=(rows, rows, rows, rows, P(), P(), P()),
        out_specs=rows,
        check_vma=False,
    )
```

```python
import functools
import math

import jax
import jax.numpy as jnp
from jax import lax
from jax.experimental import pallas as pl
from jax.experimental.pallas import tpu as pltpu
from jax.sharding import PartitionSpec as P

BLOCK = 128
SUB = 8
LEVELS = 4
CONTRACT_LAST = (((1,), (1,)), ((), ()))
CONTRACT_FIRST = (((1,), (0,)), ((), ()))


def halves(value):
    high = value.astype(jnp.bfloat16)
    low = (value - high.astype(jnp.float32)).astype(jnp.bfloat16)
    return high, low


def dot_split(left, right):
    left_high, left_low = left
    right_high, right_low = right

    def one(a, b):
        return lax.dot_general(a, b, CONTRACT_LAST, preferred_element_type=jnp.float32)

    return one(left_high, right_high) + (one(left_high, right_low) + one(left_low, right_high))


def dot_nt(left, right):
    return dot_split(halves(left), halves(right))


def spread(value, rows, columns):
    return jnp.broadcast_to(value, (rows, columns))


def diagonal_inverse(block, pause):
    count = BLOCK // SUB
    rows = [block[v * SUB : (v + 1) * SUB] for v in range(count)]
    lane = lax.broadcasted_iota(jnp.int32, (SUB, BLOCK), 1)
    sub = lax.broadcasted_iota(jnp.int32, (SUB, BLOCK), 0)
    for b in range(count):
        if b == count // 2:
            pause()
        base = b * SUB
        inside = (lane >= base) & (lane < base + SUB)
        own = rows[b]
        columns = [spread(own[:, base + j : base + j + 1], SUB, BLOCK) for j in range(SUB)]
        a = [
            [spread(columns[j][i : i + 1], SUB, BLOCK) for j in range(i + 1)] for i in range(SUB)
        ]
        inverse = []
        ratio = [[None] * SUB for _ in range(SUB)]
        for i in range(SUB):
            inverse.append(1.0 / a[i][i])
            for j in range(i + 1, SUB):
                ratio[j][i] = a[j][i] * inverse[i]
            for j in range(i + 1, SUB):
                for k in range(i + 1, j + 1):
                    a[j][k] = a[j][k] - ratio[j][i] * a[k][i]
        cleared = jnp.where(inside, 0.0, own)
        pivots = []
        for j in range(SUB):
            row = spread(cleared[j : j + 1], SUB, BLOCK)
            row = jnp.where(lane == base + j, 1.0, row)
            for i in range(j):
                row = row - ratio[j][i] * pivots[i]
            pivots.append(row)
        for v in range(b + 1, count):
            old = rows[v]
            new = jnp.where(inside, 0.0, old)
            factors = []
            for j in range(SUB):
                column = spread(old[:, base + j : base + j + 1], SUB, BLOCK)
                for i in range(j):
                    column = column - factors[i] * a[j][i]
                factors.append(column * inverse[j])
            for j in range(SUB):
                new = new - factors[j] * pivots[j]
            rows[v] = new
        final = jnp.zeros((SUB, BLOCK), jnp.float32)
        scale = jnp.ones((SUB, BLOCK), jnp.float32)
        for j in range(SUB):
            final = jnp.where(sub == j, pivots[j], final)
            scale = jnp.where(sub == j, a[j][j], scale)
        rows[b] = jnp.where(lane <= sub + base, final / jnp.sqrt(scale), 0.0)
    return jnp.concatenate(rows, axis=0)


def neighbours(level):
    leaf = lax.axis_index("leaf")
    row = lax.axis_index("row")
    partners = []
    for bit in range(level):
        flag = leaf // 2**bit % 2
        partners.append({"leaf": leaf + (1 - 2 * flag) * 2**bit, "row": row})
    count = lax.axis_size("row")
    sibling = row + 1 - 2 * (row % 2)
    forward = [lax.rem(row + 2 * d, count) for d in range(1, count // 2)]
    backward = [lax.rem(row + count - 2 * d, count) for d in range(1, count // 2)]
    across = [{"leaf": leaf, "row": other} for other in forward]
    return partners, {"leaf": leaf, "row": sibling}, across, backward


def remote(source, target, sends, receives, slot, device):
    return pltpu.make_async_remote_copy(
        src_ref=source,
        dst_ref=target,
        send_sem=sends.at[slot],
        recv_sem=receives.at[slot],
        device_id=device,
        device_id_type=pl.DeviceIdType.MESH,
    )


class Gather:
    def __init__(self, buffer, place, sends, receives, slot, near, source=None):
        _, sibling, across, origins = near
        own = buffer.at[place(lax.axis_index("row"))]
        if source is None:
            source = own
        self.direct = remote(source, own, sends, receives, slot, sibling)
        self.far = []
        self.relay = []
        for n, (device, origin) in enumerate(zip(across, origins)):
            self.far.append(remote(source, own, sends, receives, slot + 1 + 2 * n, device))
            passed = buffer.at[place(origin)]
            self.relay.append(remote(passed, passed, sends, receives, slot + 2 + 2 * n, sibling))

    def start(self):
        for copy in self.far:
            copy.start()
        self.direct.start()

    def pass_on(self):
        for copy, relay in zip(self.far, self.relay):
            copy.wait_recv()
            relay.start()

    def finish(self):
        self.direct.wait_recv()
        for relay in self.relay:
            relay.wait_recv()
        for copy in [self.direct] + self.far + self.relay:
            copy.wait_send()


def rows_at(size, base=0):
    def place(row):
        return pl.ds(pl.multiple_of(row * size + base, 8), size)

    return place


def column_tiles(order):
    count = order // BLOCK
    return [(i, j) for j in range(count) for i in range(j, count)]


def pivot_chunks(order):
    count = order // BLOCK
    return [(0, 1), (1, count), (count, 2 * count - 1), (2 * count - 1, len(column_tiles(order)))]


def dot_split_nn(left, right):
    left_high, left_low = left
    right_high, right_low = right

    def one(a, b):
        return lax.dot_general(a, b, CONTRACT_FIRST, preferred_element_type=jnp.float32)

    return one(left_high, right_high) + (one(left_high, right_low) + one(left_low, right_high))


def entry_barrier(near):
    partners, sibling, across, _ = near
    barrier = pltpu.get_barrier_semaphore()
    peers = partners + [sibling] + across
    for peer in peers:
        pl.semaphore_signal(barrier, inc=1, device_id=peer, device_id_type=pl.DeviceIdType.MESH)
    pl.semaphore_wait(barrier, len(peers))


def bit_reversed(index, bits):
    return sum((index >> b & 1) << (bits - 1 - b) for b in range(bits))


def rows_at_scaled(stride, base, size):
    def place(row):
        return pl.ds(pl.multiple_of(row * stride + base, 8), size)

    return place


class Links:
    def __init__(self, near, sends, receives):
        self.near = near
        self.sends = sends
        self.receives = receives
        self.used = 0

    def copy(self, source, target, device):
        slot = self.used
        self.used += 1
        return remote(source, target, self.sends, self.receives, slot, device)

    def gather(self, buffer, place, source=None):
        slot = self.used
        self.used += 1 + 2 * len(self.near[2])
        return Gather(buffer, place, self.sends, self.receives, slot, self.near, source)


def gather_task(move):
    return [move.start, move.pass_on, move.finish]


def sum_task(links, bits, share, span, inbox, sums, target, place):
    row = lax.axis_index("row")
    partners = links.near[0]
    moves = []
    for k, bit in enumerate(bits):
        source = share.at[span] if k == 0 else sums.at[k - 1, span]
        moves.append(links.copy(source, inbox.at[k, span], partners[bit]))
    spread = links.gather(target, place)

    def advance(k):
        moves[k].wait()
        total = (share[span] if k == 0 else sums[k - 1, span]) + inbox[k, span]
        if k + 1 < len(bits):
            sums[k, span] = total
            moves[k + 1].start()
        else:
            target[place(row)] = total
            spread.start()

    steps = [functools.partial(advance, k) for k in range(len(bits))]
    return [moves[0].start] + steps + [spread.pass_on, spread.finish]


def scatter_task(links, bits, share, start, height, inbox, sums, target, stride):
    row = lax.axis_index("row")
    leaf = lax.axis_index("leaf")
    partners = links.near[0]
    flags = [leaf // 2**bit % 2 for bit in bits]
    heights = [height // 2 ** (k + 1) for k in range(len(bits))]
    moves = []
    for k, bit in enumerate(bits):
        size = heights[k]
        other = pl.multiple_of((1 - flags[k]) * size, 8)
        if k == 0:
            source = share.at[pl.ds(start + other, size)]
        else:
            source = sums.at[k - 1, pl.ds(other, size)]
        moves.append(links.copy(source, inbox.at[k, pl.ds(0, size)], partners[bit]))
    regions = []
    origin = row * stride + start
    for flag, size in zip(flags, heights):
        origin = origin + flag * size
        regions.append(pl.ds(pl.multiple_of(origin, 8), size))
    returns = []
    for region, bit in reversed(list(zip(regions, bits))):
        returns.append(links.copy(target.at[region], target.at[region], partners[bit]))
    spread = links.gather(target, rows_at_scaled(stride, start, height))

    def reduce(k):
        size = heights[k]
        moves[k].wait()
        keep = pl.multiple_of(flags[k] * size, 8)
        mine = share[pl.ds(start + keep, size)] if k == 0 else sums[k - 1, pl.ds(keep, size)]
        total = mine + inbox[k, :size]
        if k + 1 < len(bits):
            sums[k, :size] = total
            moves[k + 1].start()
        else:
            target[regions[-1]] = total
            returns[0].start()

    def widen(k):
        returns[k].wait()
        if k + 1 < len(bits):
            returns[k + 1].start()
        else:
            spread.start()

    down = [functools.partial(reduce, k) for k in range(len(bits))]
    up = [functools.partial(widen, k) for k in range(len(bits))]
    return [moves[0].start] + down + up + [spread.pass_on, spread.finish]


def extra_task(links, bits, extra, columns, inbox, middle, final_in, result):
    leaf = lax.axis_index("leaf")
    partners = links.near[0]
    flags = [leaf // 2**bit % 2 for bit in range(LEVELS - 1)]
    size = result.shape[0]
    near, far = bits[0], bits[1]

    def pick(axis, flag):
        return (pl.ds(flag, 1), pl.ds(0, 2)) if axis == 0 else (pl.ds(0, 2), pl.ds(flag, 1))

    def inner(flag):
        return (pl.ds(0, 1), pl.ds(flag, 1)) if near == 0 else (pl.ds(flag, 1), pl.ds(0, 1))

    deep = LEVELS - 2
    half = lambda flag: pl.ds(pl.multiple_of(flag * size, 8), size)
    whole = pl.ds(0, 2 * size)
    give = extra.at[(*pick(near, 1 - flags[near]), whole, columns)]
    moves = [links.copy(give, inbox, partners[near])]
    moves.append(links.copy(middle.at[0].at[inner(1 - flags[far])], middle.at[1].at[(pl.ds(0, 1), pl.ds(0, 1))], partners[far]))
    moves.append(links.copy(final_in.at[0, half(1 - flags[deep])], final_in.at[1, pl.ds(0, size)], partners[deep]))

    def one():
        moves[0].wait()
        middle[0] = extra[(*pick(near, flags[near]), whole, columns)] + inbox[...]
        moves[1].start()

    def two():
        moves[1].wait()
        kept = middle[(0, *inner(flags[far]))] + middle[1, :1, :1]
        final_in[0] = kept.reshape(kept.shape[2:])
        moves[2].start()

    def three():
        moves[2].wait()
        result[...] = final_in[0, half(flags[deep])] + final_in[1, :size]

    return [moves[0].start, one, two, three]


def factor(diagonal, column, lower, inverse, spare, hook):
    order = lower.shape[1]
    tiles = order // BLOCK
    product, cross, block = spare
    row_ids = lax.broadcasted_iota(jnp.int32, (order, BLOCK), 0)

    def store(target, where, value):
        high, low = halves(value)
        target[(0, *where)] = high
        target[(1, *where)] = low

    def step(j, carry):
        hook(j, 0)
        start = pl.multiple_of(j * BLOCK, BLOCK)
        span = pl.ds(start, BLOCK)
        mine = lower[0, span], lower[1, span]
        product[...] = dot_split((lower[0], lower[1]), mine)
        cross[...] = dot_split_nn(mine, (inverse[0], inverse[1]))
        block[...] = diagonal_inverse(
            diagonal(j) - dot_split(mine, mine), functools.partial(hook, j, 1)
        )
        hook(j, 2)
        own = halves(block[...])
        below = jnp.where(row_ids >= start + BLOCK, column(j) - product[...], 0.0)
        store(lower, (slice(None), span), dot_split(halves(below), own))
        store(inverse, (span, slice(None)), -dot_split_nn(own, halves(cross[...])))
        inverse[0, span, span] = own[0]
        inverse[1, span, span] = own[1]
        return carry

    lax.fori_loop(0, tiles, step, 0)


def front_kernel(level, row_count, front, order, *refs):
    last = level == LEVELS - 1
    first = level == 0
    group = 2**level
    below = front - order
    count = order // BLOCK
    size = BLOCK // row_count
    refs = list(refs)
    take = lambda: refs.pop(0)
    row = lax.axis_index("row")
    member = lax.axis_index("leaf") % group
    old = kept = None
    if first:
        panel, *panels = take(), take()
    else:
        back, next_panel, fresh = take(), take(), take()
        old = take() if level > 1 else None
        panels = [take() for _ in range(LEVELS - 2)] if level == 1 else []
    result = take()
    if not first and not last:
        kept = take()
    joined = [take() for _ in panels]
    lower, inverse, product, cross, block, columns, sends, receives = [take() for _ in range(8)]
    held = [take() for _ in panels]
    near = neighbours(level)
    links = Links(near, sends, receives)
    lower[...] = jnp.zeros_like(lower)
    inverse[...] = jnp.zeros_like(inverse)
    panel_tasks = []
    for part, buffer in zip(panels, held):
        height = part.shape[0]
        panel_tasks.append(gather_task(links.gather(buffer, rows_at(height), part)))
        buffer[rows_at(height)(row)] = part[...]
    if first:
        entry_barrier(near)
        gathered = take()
        chunk = panel.shape[0]

        def piece(base, height, left, width):
            def place(index):
                return rows_at_scaled(chunk, base, height)(index), pl.ds(left, width)

            source = panel.at[pl.ds(base, height), pl.ds(left, width)]
            return gather_task(links.gather(gathered, place, source))

        step = math.gcd(chunk, BLOCK)
        strips = [piece(base, step, 0, BLOCK) for base in range(0, chunk, step)]
        strips += [piece(0, chunk, left, BLOCK) for left in range(BLOCK, order, BLOCK)]
        for strip in strips:
            strip[0]()
        own = pl.ds(pl.multiple_of(row * chunk, 8), chunk)
        gathered[own] = panel[...]
        panel_tasks[0][0]()
        lead = chunk // step
        early = BLOCK // step
        for stage in (1, 2):
            for strip in strips[:early]:
                strip[stage]()
        rest = strips[early:lead]
        plan = {(0, 1): [s[1] for s in rest], (0, 2): [s[2] for s in rest]}
        for n, strip in enumerate(strips[lead:]):
            plan[n, 2] = plan.get((n, 2), []) + [strip[1]]
            plan[n + 1, 0] = [strip[2]]
        plan[count - 1, 2] = [panel_tasks[0][1]]
        after = []
        finally_ = panel_tasks[0][2:]

        def diagonal(j):
            span = pl.ds(pl.multiple_of(j * BLOCK, BLOCK), BLOCK)
            return gathered[span, span]

        def column(j):
            return gathered[:order, pl.ds(pl.multiple_of(j * BLOCK, BLOCK), BLOCK)]

    else:
        packed, pivot_share, pivot_sum, pivot_in = [take() for _ in range(4)]
        below_share, below_sum, below_in, placed, whole_panel = [take() for _ in range(5)]
        tasks = []
        turns = [list(range(level)), list(range(level))]
        if level > 1:
            turns[1][0], turns[1][1] = 1, 0
        for n, (begin, end) in enumerate(pivot_chunks(order)):

            def place(index, begin=begin, end=end):
                return pl.ds(begin, end - begin), pl.ds(pl.multiple_of(index * size, 8), size)

            bits = turns[n % 2] if n else turns[0]
            span = pl.ds(begin, end - begin)
            tasks.append(
                sum_task(links, bits, pivot_share, span, pivot_in, pivot_sum, packed, place)
            )
        share = below_share.shape[0]
        parts = 2 if last else 4
        height = share // parts
        for n in range(parts):
            if last:
                tasks.append(
                    scatter_task(
                        links, turns[n], below_share, n * height, height, below_in.at[n],
                        below_sum.at[n], columns, share,
                    )
                )
            else:
                tasks.append(
                    sum_task(
                        links, turns[n % 2], below_share, pl.ds(n * height, height), below_in,
                        below_sum, columns, rows_at_scaled(share, n * height, height),
                    )
                )
        a, b, c, d, e, f, *more = tasks
        both = lambda k: [e[k], f[k]]

        def fetch(i):
            target = slice(i * BLOCK, (i + 1) * BLOCK)
            depth = 0 if old is None else old.shape[2]
            if depth:
                placed[target, :depth] = old[back[i]]
            placed[target, depth:] = fresh[back[i]]

        whole_panel[...] = jnp.zeros_like(whole_panel)
        held_rows = next_panel.shape[0]
        whole_panel[pl.ds(pl.multiple_of(member * held_rows, 8), held_rows)] = next_panel[...]
        for i in range(front // BLOCK):
            fetch(i)
        entry_barrier(near)
        pivots = halves(placed[:order])
        mine = [pl.ds(pl.multiple_of(i * BLOCK + row * size, 8), size) for i in range(count)]
        own = halves(jnp.concatenate([placed[span] for span in mine], axis=0))
        part = dot_split(own, pivots)
        for t, (i, j) in enumerate(column_tiles(order)):
            along = slice(j * BLOCK, (j + 1) * BLOCK)
            pivot_share[t] = whole_panel[mine[i], along] - part[i * size : (i + 1) * size, along]
        for task in (a, b, c, d):
            task[0]()
        spot = rows_at_scaled(share, order, share)(row)
        below_share[...] = whole_panel[spot] - dot_split(halves(placed[spot]), pivots)
        for task in [e, f] + more:
            task[0]()

        def keep():
            kept[: below // BLOCK] = placed[order:].reshape(below // BLOCK, *kept.shape[1:])
            kept[below // BLOCK] = jnp.zeros(kept.shape[1:], jnp.float32)

        finally_ = []
        if level == 1:
            g, h = more
            pre = [a[1], b[1], a[2], c[1], d[1]] + [t[0] for t in panel_tasks] + [keep, b[2], a[3]]
            plan = {
                (0, 1): [c[2], d[2], e[1]],
                (0, 2): [b[3]],
                (1, 0): [c[3], f[1]],
                (1, 1): [d[3], g[1]],
                (1, 2): [h[1], e[2]],
                (2, 1): [f[2], e[3]] + [t[1] for t in panel_tasks],
                (2, 2): [g[2]],
                (3, 0): [f[3]],
                (3, 1): [h[2], g[3]],
            }
            after = [h[3]]
            finally_ = [t[2] for t in panel_tasks]
        elif level == 2:
            g, h = more
            pre = [a[1], b[1], c[1], d[1], keep, a[2], b[2], c[2], d[2], e[1], f[1]]
            pre += [a[3], b[3], a[4]]
            plan = {
                (0, 1): [c[3], d[3], g[1], h[1]],
                (0, 2): [b[4]],
                (1, 0): [c[4], e[2], f[2]],
                (1, 1): [d[4]],
                (1, 2): [g[2], h[2], e[3]],
                (2, 1): [f[3], e[4]],
                (3, 0): [g[3]],
                (3, 1): [f[4], h[3]],
                (3, 2): [g[4]],
            }
            after = [h[4]]
        else:
            extra, inbox0, middle0, final0, inbox1, middle1, final1, sums0, sums1 = [
                take() for _ in range(9)
            ]
            half = below // 2
            x = extra_task(links, (0, 1), extra, pl.ds(0, half), inbox0, middle0, final0, sums0)
            y = extra_task(links, (1, 0), extra, pl.ds(half, half), inbox1, middle1, final1, sums1)

            def begin_extra():
                height = result.shape[0]
                rows = [None] * group
                for index in range(group):
                    start = pl.multiple_of(order + (index * row_count + row) * height, 8)
                    rows[bit_reversed(index, LEVELS - 1)] = placed[pl.ds(start, height)]
                part = halves(jnp.concatenate(rows, axis=0))
                for left, task in ((0, x), (half, y)):
                    other = halves(placed[order + left : order + left + half])
                    value = -dot_split(part, other)
                    extra[..., left : left + half] = value.reshape(*extra.shape[:3], half)
                    task[0]()

            pre = [a[1], b[1], c[1], d[1], begin_extra, a[2], b[2], c[2], d[2]] + both(1)
            pre += [a[3], b[3], a[4], c[3], d[3], b[4], a[5]]
            plan = {
                (0, 1): both(2) + [c[4], d[4]],
                (0, 2): [b[5]],
                (1, 0): [c[5]] + both(3),
                (1, 1): [x[1], y[1]] + both(4),
                (2, 0): [d[5]] + both(5),
                (2, 1): [x[2], y[2]],
                (2, 2): both(6),
                (3, 1): [x[3], y[3]],
                (3, 2): [e[7]],
            }
            after = [f[7], e[8], f[8]]
        for action in pre:
            action()

        def diagonal(j):
            return packed[j * count - j * (j - 1) // 2]

        def column(j):
            start = j * count - j * (j - 1) // 2 - j
            return packed[pl.ds(start, count)].reshape(order, BLOCK)

    def hook(j, slot):
        for (when, which), actions in plan.items():
            if which == slot:

                @pl.when(j == when)
                def _():
                    for action in actions:
                        action()

    factor(diagonal, column, lower, inverse, (product, cross, block), hook)
    for action in after:
        action()
    if last:
        height = result.shape[0]
        position = member * row_count + row
        own = columns[pl.ds(pl.multiple_of(position * height, 8), height)]
        whole = inverse[0], inverse[1]
        weight = dot_split_nn(halves(dot_split(halves(own), whole)), whole)
        rest = dot_nt(weight, columns[...])
        result[:, :half] = sums0[...] - rest[:, :half]
        result[:, half:] = sums1[...] - rest[:, half:]
        return
    width = order // group
    blocks = below // BLOCK
    if first:
        for left in range(0, order, 2 * BLOCK):
            right = min(left + 2 * BLOCK, order)
            part = inverse[0, left:right, :right], inverse[1, left:right, :right]
            value = dot_split(halves(gathered[order:, :right]), part)
            result[:blocks, :, left:right] = value.reshape(blocks, BLOCK, right - left)
    else:
        span = pl.ds(pl.multiple_of(member * width, BLOCK), width)
        value = dot_split(halves(columns[...]), (inverse[0, span], inverse[1, span]))
        result[:blocks] = value.reshape(blocks, BLOCK, width)
    result[blocks] = jnp.zeros((BLOCK, width), jnp.float32)
    for action in finally_:
        action()
    for buffer, target in zip(held, joined):
        target[...] = buffer[...]


def front_step(level, row_count, front, order, operands, panels):
    below = front - order
    width = order // 2**level
    tiles = len(column_tiles(order))
    float32 = jnp.float32

    def vmem(*shape, dtype=float32):
        return pltpu.VMEM(shape, dtype)

    def out(*shape):
        return jax.ShapeDtypeStruct(shape, float32)

    last = level == LEVELS - 1
    rest = below // row_count
    top = 2 ** (LEVELS - 1)
    copies = 8 * (row_count - 1) + 32
    scratch = [
        vmem(2, order, order, dtype=jnp.bfloat16),
        vmem(2, order, order, dtype=jnp.bfloat16),
        vmem(order, BLOCK),
        vmem(BLOCK, order),
        vmem(BLOCK, BLOCK),
        vmem(below if level else 8, order),
        pltpu.SemaphoreType.DMA((copies,)),
        pltpu.SemaphoreType.DMA((copies,)),
    ]
    heights = [row_count * panel.shape[0] for panel in panels]
    scratch += [vmem(height, order) for height in heights]
    depth = sum(order // 2**k for k in range(level))
    if level == 0:
        scratch.append(vmem(front, order))
    else:
        share = (tiles, BLOCK // row_count, BLOCK)
        scratch += [vmem(tiles, BLOCK, BLOCK), vmem(*share), vmem(level, *share), vmem(level, *share)]
        scratch.append(vmem(rest, order))
        if last:
            scratch += [vmem(2, level, rest // 4, order), vmem(2, level, rest // 4, order)]
        else:
            scratch += [vmem(level, rest, order), vmem(level, rest, order)]
        scratch += [vmem(front, depth), vmem(front, order)]
    if last:
        height = rest // top
        half = below // 2
        scratch.append(vmem(2, 2, 2 * height, below))
        for shape in ((1, 2), (2, 1)):
            scratch += [
                vmem(*shape, 2 * height, half),
                vmem(2, *shape, 2 * height, half),
                vmem(2, 2 * height, half),
            ]
        scratch += [vmem(height, half), vmem(height, half)]
        shapes = out(height, below)
    else:
        blocks = below // BLOCK + 1
        shapes = [out(blocks, BLOCK, width)]
        if level:
            shapes.append(out(blocks, BLOCK, depth))
        shapes += [out(height, order) for height in heights]
    operands = operands + panels
    specs = [pl.BlockSpec(memory_space=pltpu.VMEM)] * len(operands)
    if level:
        specs[0] = pl.BlockSpec(memory_space=pltpu.SMEM)
    return pl.pallas_call(
        functools.partial(front_kernel, level, row_count, front, order),
        out_shape=shapes,
        in_specs=specs,
        scratch_shapes=scratch,
        name=f"front{level}",
        compiler_params=pltpu.CompilerParams(
            vmem_limit_bytes=60 * 2**20, collective_id=level, has_side_effects=True
        ),
    )(*operands)


def body(panel0, panel1, panel2, panel3, maps1, maps2, maps3):
    block_maps = (maps1, maps2, maps3)
    row_count = lax.axis_size("row")
    leaf = lax.axis_index("leaf")
    order = panel0.shape[1]
    front = panel0.shape[0] * row_count
    parents = front // BLOCK
    children = (front - order) // BLOCK
    operands = [panel0]
    waiting = [[panel1], [panel2, panel3], [], []]
    panels = []
    for level in range(LEVELS):
        outs = front_step(level, row_count, front, order, operands, waiting[level])
        if level == LEVELS - 1:
            return outs
        blocks = lax.dynamic_index_in_dim(block_maps[level], leaf // 2**level, 0, keepdims=False)
        hit = blocks[None, :] == jnp.arange(parents, dtype=jnp.int32)[:, None]
        back = jnp.min(
            jnp.where(hit, jnp.arange(children, dtype=jnp.int32)[None, :], children), axis=1
        )
        data = outs[: 2 if level else 1]
        panels += outs[len(data) :]
        operands = [back, panels[level], *data]


def solution(mesh):
    rows = P(("leaf", "row"), None)
    return jax.shard_map(
        body,
        mesh=mesh,
        in_specs=(rows, rows, rows, rows, P(), P(), P()),
        out_specs=rows,
        check_vma=False,
    )
```

```python
import functools
import math

import jax
import jax.numpy as jnp
from jax import lax
from jax.experimental import pallas as pl
from jax.experimental.pallas import tpu as pltpu
from jax.sharding import PartitionSpec as P

BLOCK = 128
SUB = 8
LEVELS = 4
CONTRACT_LAST = (((1,), (1,)), ((), ()))
CONTRACT_FIRST = (((1,), (0,)), ((), ()))


def halves(value):
    high = value.astype(jnp.bfloat16)
    low = (value - high.astype(jnp.float32)).astype(jnp.bfloat16)
    return high, low


def dot_split(left, right):
    left_high, left_low = left
    right_high, right_low = right

    def one(a, b):
        return lax.dot_general(a, b, CONTRACT_LAST, preferred_element_type=jnp.float32)

    return one(left_high, right_high) + (one(left_high, right_low) + one(left_low, right_high))


def dot_nt(left, right):
    return dot_split(halves(left), halves(right))


def spread(value, rows, columns):
    return jnp.broadcast_to(value, (rows, columns))


def diagonal_inverse(block, nothing, pause):
    count = BLOCK // SUB
    rows = [block[v * SUB : (v + 1) * SUB] for v in range(count)]
    lane = lax.broadcasted_iota(jnp.int32, (SUB, BLOCK), 1)
    sub = lax.broadcasted_iota(jnp.int32, (SUB, BLOCK), 0)
    for b in range(count):
        if b == count // 2:
            pause()
        base = b * SUB
        inside = (lane >= base) & (lane < base + SUB)
        own = rows[b]
        columns = [
            spread(own[:, base + j : base + j + 1], SUB, BLOCK) + nothing for j in range(SUB)
        ]
        a = [
            [spread(columns[j][i : i + 1], SUB, BLOCK) for j in range(i + 1)] for i in range(SUB)
        ]
        inverse = []
        ratio = [[None] * SUB for _ in range(SUB)]
        for i in range(SUB):
            inverse.append(1.0 / a[i][i])
            for j in range(i + 1, SUB):
                ratio[j][i] = a[j][i] * inverse[i]
            for j in range(i + 1, SUB):
                for k in range(i + 1, j + 1):
                    a[j][k] = a[j][k] - ratio[j][i] * a[k][i]
        cleared = jnp.where(inside, 0.0, own)
        pivots = []
        for j in range(SUB):
            row = spread(cleared[j : j + 1], SUB, BLOCK)
            row = jnp.where(lane == base + j, 1.0, row)
            for i in range(j):
                row = row - ratio[j][i] * pivots[i]
            pivots.append(row)
        for v in range(b + 1, count):
            old = rows[v]
            new = jnp.where(inside, 0.0, old)
            factors = []
            for j in range(SUB):
                column = spread(old[:, base + j : base + j + 1], SUB, BLOCK)
                for i in range(j):
                    column = column - factors[i] * a[j][i]
                factors.append(column * inverse[j])
            for j in range(SUB):
                new = new - factors[j] * pivots[j]
            rows[v] = new
        final = jnp.zeros((SUB, BLOCK), jnp.float32)
        scale = jnp.ones((SUB, BLOCK), jnp.float32)
        for j in range(SUB):
            final = jnp.where(sub == j, pivots[j], final)
            scale = jnp.where(sub == j, a[j][j], scale)
        rows[b] = jnp.where(lane <= sub + base, final / jnp.sqrt(scale), 0.0)
    return jnp.concatenate(rows, axis=0)


def neighbours(level):
    leaf = lax.axis_index("leaf")
    row = lax.axis_index("row")
    partners = []
    for bit in range(level):
        flag = leaf // 2**bit % 2
        partners.append({"leaf": leaf + (1 - 2 * flag) * 2**bit, "row": row})
    count = lax.axis_size("row")
    sibling = row + 1 - 2 * (row % 2)
    forward = [lax.rem(row + 2 * d, count) for d in range(1, count // 2)]
    backward = [lax.rem(row + count - 2 * d, count) for d in range(1, count // 2)]
    across = [{"leaf": leaf, "row": other} for other in forward]
    return partners, {"leaf": leaf, "row": sibling}, across, backward


def remote(source, target, sends, receives, slot, device):
    return pltpu.make_async_remote_copy(
        src_ref=source,
        dst_ref=target,
        send_sem=sends.at[slot],
        recv_sem=receives.at[slot],
        device_id=device,
        device_id_type=pl.DeviceIdType.MESH,
    )


class Gather:
    def __init__(self, buffer, place, sends, receives, slot, near, source=None):
        _, sibling, across, origins = near
        own = buffer.at[place(lax.axis_index("row"))]
        if source is None:
            source = own
        self.direct = remote(source, own, sends, receives, slot, sibling)
        self.far = []
        self.relay = []
        for n, (device, origin) in enumerate(zip(across, origins)):
            self.far.append(remote(source, own, sends, receives, slot + 1 + 2 * n, device))
            passed = buffer.at[place(origin)]
            self.relay.append(remote(passed, passed, sends, receives, slot + 2 + 2 * n, sibling))

    def start(self):
        for copy in self.far:
            copy.start()
        self.direct.start()

    def pass_on(self):
        for copy, relay in zip(self.far, self.relay):
            copy.wait_recv()
            relay.start()

    def finish(self):
        self.direct.wait_recv()
        for relay in self.relay:
            relay.wait_recv()
        for copy in [self.direct] + self.far + self.relay:
            copy.wait_send()


def rows_at(size, base=0):
    def place(row):
        return pl.ds(pl.multiple_of(row * size + base, 8), size)

    return place


def column_tiles(order):
    count = order // BLOCK
    return [(i, j) for j in range(count) for i in range(j, count)]


def pivot_chunks(order):
    count = order // BLOCK
    return [(0, 1), (1, count), (count, 2 * count - 1), (2 * count - 1, len(column_tiles(order)))]


def dot_split_nn(left, right):
    left_high, left_low = left
    right_high, right_low = right

    def one(a, b):
        return lax.dot_general(a, b, CONTRACT_FIRST, preferred_element_type=jnp.float32)

    return one(left_high, right_high) + (one(left_high, right_low) + one(left_low, right_high))


def entry_barrier(near):
    partners, sibling, across, _ = near
    barrier = pltpu.get_barrier_semaphore()
    peers = partners + [sibling] + across
    for peer in peers:
        pl.semaphore_signal(barrier, inc=1, device_id=peer, device_id_type=pl.DeviceIdType.MESH)
    pl.semaphore_wait(barrier, len(peers))


def bit_reversed(index, bits):
    return sum((index >> b & 1) << (bits - 1 - b) for b in range(bits))


def rows_at_scaled(stride, base, size):
    def place(row):
        return pl.ds(pl.multiple_of(row * stride + base, 8), size)

    return place


class Links:
    def __init__(self, near, sends, receives):
        self.near = near
        self.sends = sends
        self.receives = receives
        self.used = 0

    def copy(self, source, target, device):
        slot = self.used
        self.used += 1
        return remote(source, target, self.sends, self.receives, slot, device)

    def gather(self, buffer, place, source=None):
        slot = self.used
        self.used += 1 + 2 * len(self.near[2])
        return Gather(buffer, place, self.sends, self.receives, slot, self.near, source)


def gather_task(move):
    return [move.start, move.pass_on, move.finish]


def sum_task(links, bits, share, span, inbox, sums, target, place):
    row = lax.axis_index("row")
    partners = links.near[0]
    moves = []
    for k, bit in enumerate(bits):
        source = share.at[span] if k == 0 else sums.at[k - 1, span]
        moves.append(links.copy(source, inbox.at[k, span], partners[bit]))
    spread = links.gather(target, place)

    def advance(k):
        moves[k].wait()
        total = (share[span] if k == 0 else sums[k - 1, span]) + inbox[k, span]
        if k + 1 < len(bits):
            sums[k, span] = total
            moves[k + 1].start()
        else:
            target[place(row)] = total
            spread.start()

    steps = [functools.partial(advance, k) for k in range(len(bits))]
    return [moves[0].start] + steps + [spread.pass_on, spread.finish]


def scatter_task(links, bits, share, start, height, inbox, sums, target, stride):
    row = lax.axis_index("row")
    leaf = lax.axis_index("leaf")
    partners = links.near[0]
    flags = [leaf // 2**bit % 2 for bit in bits]
    heights = [height // 2 ** (k + 1) for k in range(len(bits))]
    moves = []
    for k, bit in enumerate(bits):
        size = heights[k]
        other = pl.multiple_of((1 - flags[k]) * size, 8)
        if k == 0:
            source = share.at[pl.ds(start + other, size)]
        else:
            source = sums.at[k - 1, pl.ds(other, size)]
        moves.append(links.copy(source, inbox.at[k, pl.ds(0, size)], partners[bit]))
    regions = []
    origin = row * stride + start
    for flag, size in zip(flags, heights):
        origin = origin + flag * size
        regions.append(pl.ds(pl.multiple_of(origin, 8), size))
    returns = []
    for region, bit in reversed(list(zip(regions, bits))):
        returns.append(links.copy(target.at[region], target.at[region], partners[bit]))
    spread = links.gather(target, rows_at_scaled(stride, start, height))

    def reduce(k):
        size = heights[k]
        moves[k].wait()
        keep = pl.multiple_of(flags[k] * size, 8)
        mine = share[pl.ds(start + keep, size)] if k == 0 else sums[k - 1, pl.ds(keep, size)]
        total = mine + inbox[k, :size]
        if k + 1 < len(bits):
            sums[k, :size] = total
            moves[k + 1].start()
        else:
            target[regions[-1]] = total
            returns[0].start()

    def widen(k):
        returns[k].wait()
        if k + 1 < len(bits):
            returns[k + 1].start()
        else:
            spread.start()

    down = [functools.partial(reduce, k) for k in range(len(bits))]
    up = [functools.partial(widen, k) for k in range(len(bits))]
    return [moves[0].start] + down + up + [spread.pass_on, spread.finish]


def extra_task(links, bits, extra, columns, inbox, middle, final_in, result):
    leaf = lax.axis_index("leaf")
    partners = links.near[0]
    flags = [leaf // 2**bit % 2 for bit in range(LEVELS - 1)]
    size = result.shape[0]
    near, far = bits[0], bits[1]

    def pick(axis, flag):
        return (pl.ds(flag, 1), pl.ds(0, 2)) if axis == 0 else (pl.ds(0, 2), pl.ds(flag, 1))

    def inner(flag):
        return (pl.ds(0, 1), pl.ds(flag, 1)) if near == 0 else (pl.ds(flag, 1), pl.ds(0, 1))

    deep = LEVELS - 2
    half = lambda flag: pl.ds(pl.multiple_of(flag * size, 8), size)
    whole = pl.ds(0, 2 * size)
    give = extra.at[(*pick(near, 1 - flags[near]), whole, columns)]
    moves = [links.copy(give, inbox, partners[near])]
    moves.append(links.copy(middle.at[0].at[inner(1 - flags[far])], middle.at[1].at[(pl.ds(0, 1), pl.ds(0, 1))], partners[far]))
    moves.append(links.copy(final_in.at[0, half(1 - flags[deep])], final_in.at[1, pl.ds(0, size)], partners[deep]))

    def one():
        moves[0].wait()
        middle[0] = extra[(*pick(near, flags[near]), whole, columns)] + inbox[...]
        moves[1].start()

    def two():
        moves[1].wait()
        kept = middle[(0, *inner(flags[far]))] + middle[1, :1, :1]
        final_in[0] = kept.reshape(kept.shape[2:])
        moves[2].start()

    def three():
        moves[2].wait()
        result[...] = final_in[0, half(flags[deep])] + final_in[1, :size]

    return [moves[0].start, one, two, three]


def factor(diagonal, column, lower, inverse, spare, hook):
    order = lower.shape[1]
    tiles = order // BLOCK
    product, cross, block, zeros = spare
    row_ids = lax.broadcasted_iota(jnp.int32, (order, BLOCK), 0)

    def store(target, where, value):
        high, low = halves(value)
        target[(0, *where)] = high
        target[(1, *where)] = low

    def step(j, carry):
        hook(j, 0)
        start = pl.multiple_of(j * BLOCK, BLOCK)
        span = pl.ds(start, BLOCK)
        mine = lower[0, span], lower[1, span]
        product[...] = dot_split((lower[0], lower[1]), mine)
        cross[...] = dot_split_nn(mine, (inverse[0], inverse[1]))
        block[...] = diagonal_inverse(
            diagonal(j) - dot_split(mine, mine), zeros[...], functools.partial(hook, j, 1)
        )
        hook(j, 2)
        own = halves(block[...])
        below = jnp.where(row_ids >= start + BLOCK, column(j) - product[...], 0.0)
        store(lower, (slice(None), span), dot_split(halves(below), own))
        store(inverse, (span, slice(None)), -dot_split_nn(own, halves(cross[...])))
        inverse[0, span, span] = own[0]
        inverse[1, span, span] = own[1]
        return carry

    lax.fori_loop(0, tiles, step, 0)


def front_kernel(level, row_count, front, order, *refs):
    last = level == LEVELS - 1
    first = level == 0
    group = 2**level
    below = front - order
    count = order // BLOCK
    size = BLOCK // row_count
    refs = list(refs)
    take = lambda: refs.pop(0)
    row = lax.axis_index("row")
    member = lax.axis_index("leaf") % group
    old = kept = None
    if first:
        panel, *panels = take(), take()
    else:
        back, next_panel, fresh = take(), take(), take()
        old = take() if level > 1 else None
        panels = [take() for _ in range(LEVELS - 2)] if level == 1 else []
    result = take()
    if not first and not last:
        kept = take()
    joined = [take() for _ in panels]
    lower, inverse, product, cross, block, zeros = [take() for _ in range(6)]
    columns, sends, receives = [take() for _ in range(3)]
    held = [take() for _ in panels]
    near = neighbours(level)
    links = Links(near, sends, receives)
    lower[...] = jnp.zeros_like(lower)
    inverse[...] = jnp.zeros_like(inverse)
    zeros[...] = jnp.zeros_like(zeros)
    panel_tasks = []
    for part, buffer in zip(panels, held):
        height = part.shape[0]
        panel_tasks.append(gather_task(links.gather(buffer, rows_at(height), part)))
        buffer[rows_at(height)(row)] = part[...]
    if first:
        entry_barrier(near)
        gathered = take()
        chunk = panel.shape[0]

        def piece(base, height, left, width):
            def place(index):
                return rows_at_scaled(chunk, base, height)(index), pl.ds(left, width)

            source = panel.at[pl.ds(base, height), pl.ds(left, width)]
            return gather_task(links.gather(gathered, place, source))

        step = math.gcd(chunk, BLOCK)
        strips = [piece(base, step, 0, BLOCK) for base in range(0, chunk, step)]
        strips += [piece(0, chunk, left, BLOCK) for left in range(BLOCK, order, BLOCK)]
        for strip in strips:
            strip[0]()
        own = pl.ds(pl.multiple_of(row * chunk, 8), chunk)
        gathered[own] = panel[...]
        panel_tasks[0][0]()
        lead = chunk // step
        early = BLOCK // step
        for stage in (1, 2):
            for strip in strips[:early]:
                strip[stage]()
        rest = strips[early:lead]
        plan = {(0, 1): [s[1] for s in rest], (0, 2): [s[2] for s in rest]}
        for n, strip in enumerate(strips[lead:]):
            plan[n, 2] = plan.get((n, 2), []) + [strip[1]]
            plan[n + 1, 0] = [strip[2]]
        plan[count - 1, 2] = [panel_tasks[0][1]]
        after = []
        finally_ = panel_tasks[0][2:]

        def diagonal(j):
            span = pl.ds(pl.multiple_of(j * BLOCK, BLOCK), BLOCK)
            return gathered[span, span]

        def column(j):
            return gathered[:order, pl.ds(pl.multiple_of(j * BLOCK, BLOCK), BLOCK)]

    else:
        packed, pivot_share, pivot_sum, pivot_in = [take() for _ in range(4)]
        below_share, below_sum, below_in, placed, whole_panel = [take() for _ in range(5)]
        tasks = []
        turns = [list(range(level)), list(range(level))]
        if level > 1:
            turns[1][0], turns[1][1] = 1, 0
        for n, (begin, end) in enumerate(pivot_chunks(order)):

            def place(index, begin=begin, end=end):
                return pl.ds(begin, end - begin), pl.ds(pl.multiple_of(index * size, 8), size)

            bits = turns[n % 2] if n else turns[0]
            span = pl.ds(begin, end - begin)
            tasks.append(
                sum_task(links, bits, pivot_share, span, pivot_in, pivot_sum, packed, place)
            )
        share = below_share.shape[0]
        parts = 2 if last else 4
        height = share // parts
        for n in range(parts):
            if last:
                tasks.append(
                    scatter_task(
                        links, turns[n], below_share, n * height, height, below_in.at[n],
                        below_sum.at[n], columns, share,
                    )
                )
            else:
                tasks.append(
                    sum_task(
                        links, turns[n % 2], below_share, pl.ds(n * height, height), below_in,
                        below_sum, columns, rows_at_scaled(share, n * height, height),
                    )
                )
        a, b, c, d, e, f, *more = tasks
        both = lambda k: [e[k], f[k]]

        def fetch(i):
            target = slice(i * BLOCK, (i + 1) * BLOCK)
            depth = 0 if old is None else old.shape[2]
            if depth:
                placed[target, :depth] = old[back[i]]
            placed[target, depth:] = fresh[back[i]]

        whole_panel[...] = jnp.zeros_like(whole_panel)
        held_rows = next_panel.shape[0]
        whole_panel[pl.ds(pl.multiple_of(member * held_rows, 8), held_rows)] = next_panel[...]
        for i in range(front // BLOCK):
            fetch(i)
        entry_barrier(near)
        pivots = halves(placed[:order])
        mine = [pl.ds(pl.multiple_of(i * BLOCK + row * size, 8), size) for i in range(count)]
        own = halves(jnp.concatenate([placed[span] for span in mine], axis=0))
        part = dot_split(own, pivots)
        for t, (i, j) in enumerate(column_tiles(order)):
            along = slice(j * BLOCK, (j + 1) * BLOCK)
            pivot_share[t] = whole_panel[mine[i], along] - part[i * size : (i + 1) * size, along]
        for task in (a, b, c, d):
            task[0]()
        spot = rows_at_scaled(share, order, share)(row)
        below_share[...] = whole_panel[spot] - dot_split(halves(placed[spot]), pivots)
        for task in [e, f] + more:
            task[0]()

        def keep():
            kept[: below // BLOCK] = placed[order:].reshape(below // BLOCK, *kept.shape[1:])
            kept[below // BLOCK] = jnp.zeros(kept.shape[1:], jnp.float32)

        finally_ = []
        if level == 1:
            g, h = more
            pre = [a[1], b[1], a[2], c[1], d[1]] + [t[0] for t in panel_tasks] + [keep, b[2], a[3]]
            plan = {
                (0, 1): [c[2], d[2], e[1]],
                (0, 2): [b[3]],
                (1, 0): [c[3], f[1]],
                (1, 1): [d[3], g[1]],
                (1, 2): [h[1], e[2]],
                (2, 1): [f[2], e[3]] + [t[1] for t in panel_tasks],
                (2, 2): [g[2]],
                (3, 0): [f[3]],
                (3, 1): [h[2], g[3]],
            }
            after = [h[3]]
            finally_ = [t[2] for t in panel_tasks]
        elif level == 2:
            g, h = more
            pre = [a[1], b[1], c[1], d[1], keep, a[2], b[2], c[2], d[2], e[1], f[1]]
            pre += [a[3], b[3], a[4]]
            plan = {
                (0, 1): [c[3], d[3], g[1], h[1]],
                (0, 2): [b[4]],
                (1, 0): [c[4], e[2], f[2]],
                (1, 1): [d[4]],
                (1, 2): [g[2], h[2], e[3]],
                (2, 1): [f[3], e[4]],
                (3, 0): [g[3]],
                (3, 1): [f[4], h[3]],
                (3, 2): [g[4]],
            }
            after = [h[4]]
        else:
            extra, inbox0, middle0, final0, inbox1, middle1, final1, sums0, sums1 = [
                take() for _ in range(9)
            ]
            half = below // 2
            x = extra_task(links, (0, 1), extra, pl.ds(0, half), inbox0, middle0, final0, sums0)
            y = extra_task(links, (1, 0), extra, pl.ds(half, half), inbox1, middle1, final1, sums1)

            def begin_extra():
                height = result.shape[0]
                rows = [None] * group
                for index in range(group):
                    start = pl.multiple_of(order + (index * row_count + row) * height, 8)
                    rows[bit_reversed(index, LEVELS - 1)] = placed[pl.ds(start, height)]
                part = halves(jnp.concatenate(rows, axis=0))
                for left, task in ((0, x), (half, y)):
                    other = halves(placed[order + left : order + left + half])
                    value = -dot_split(part, other)
                    extra[..., left : left + half] = value.reshape(*extra.shape[:3], half)
                    task[0]()

            pre = [a[1], b[1], a[2], b[2], c[1], d[1]] + both(1) + [c[2], d[2], begin_extra]
            pre += [a[3], b[3]] + both(2) + [a[4], c[3], d[3], b[4], a[5]]
            plan = {
                (0, 1): both(3) + [c[4], d[4]],
                (0, 2): [b[5]],
                (1, 0): [c[5]] + both(4),
                (1, 1): both(5),
                (1, 2): both(6),
                (2, 0): [d[5], x[1], y[1]],
                (2, 2): [x[2], y[2]],
                (3, 1): [e[7]],
                (3, 2): [e[8]],
            }
            after = [x[3], y[3], f[7], f[8]]
        for action in pre:
            action()

        def diagonal(j):
            return packed[j * count - j * (j - 1) // 2]

        def column(j):
            start = j * count - j * (j - 1) // 2 - j
            return packed[pl.ds(start, count)].reshape(order, BLOCK)

    def hook(j, slot):
        for (when, which), actions in plan.items():
            if which == slot:

                @pl.when(j == when)
                def _():
                    for action in actions:
                        action()

    factor(diagonal, column, lower, inverse, (product, cross, block, zeros), hook)
    for action in after:
        action()
    if last:
        height = result.shape[0]
        position = member * row_count + row
        own = columns[pl.ds(pl.multiple_of(position * height, 8), height)]
        whole = inverse[0], inverse[1]
        weight = dot_split_nn(halves(dot_split(halves(own), whole)), whole)
        rest = dot_nt(weight, columns[...])
        result[:, :half] = sums0[...] - rest[:, :half]
        result[:, half:] = sums1[...] - rest[:, half:]
        return
    width = order // group
    blocks = below // BLOCK
    if first:
        for left in range(0, order, 2 * BLOCK):
            right = min(left + 2 * BLOCK, order)
            part = inverse[0, left:right, :right], inverse[1, left:right, :right]
            value = dot_split(halves(gathered[order:, :right]), part)
            result[:blocks, :, left:right] = value.reshape(blocks, BLOCK, right - left)
    else:
        span = pl.ds(pl.multiple_of(member * width, BLOCK), width)
        value = dot_split(halves(columns[...]), (inverse[0, span], inverse[1, span]))
        result[:blocks] = value.reshape(blocks, BLOCK, width)
    result[blocks] = jnp.zeros((BLOCK, width), jnp.float32)
    for action in finally_:
        action()
    for buffer, target in zip(held, joined):
        target[...] = buffer[...]


def front_step(level, row_count, front, order, operands, panels):
    below = front - order
    width = order // 2**level
    tiles = len(column_tiles(order))
    float32 = jnp.float32

    def vmem(*shape, dtype=float32):
        return pltpu.VMEM(shape, dtype)

    def out(*shape):
        return jax.ShapeDtypeStruct(shape, float32)

    last = level == LEVELS - 1
    rest = below // row_count
    top = 2 ** (LEVELS - 1)
    copies = 8 * (row_count - 1) + 32
    scratch = [
        vmem(2, order, order, dtype=jnp.bfloat16),
        vmem(2, order, order, dtype=jnp.bfloat16),
        vmem(order, BLOCK),
        vmem(BLOCK, order),
        vmem(BLOCK, BLOCK),
        vmem(SUB, BLOCK),
        vmem(below if level else 8, order),
        pltpu.SemaphoreType.DMA((copies,)),
        pltpu.SemaphoreType.DMA((copies,)),
    ]
    heights = [row_count * panel.shape[0] for panel in panels]
    scratch += [vmem(height, order) for height in heights]
    depth = sum(order // 2**k for k in range(level))
    if level == 0:
        scratch.append(vmem(front, order))
    else:
        share = (tiles, BLOCK // row_count, BLOCK)
        scratch += [vmem(tiles, BLOCK, BLOCK), vmem(*share), vmem(level, *share), vmem(level, *share)]
        scratch.append(vmem(rest, order))
        if last:
            scratch += [vmem(2, level, rest // 4, order), vmem(2, level, rest // 4, order)]
        else:
            scratch += [vmem(level, rest, order), vmem(level, rest, order)]
        scratch += [vmem(front, depth), vmem(front, order)]
    if last:
        height = rest // top
        half = below // 2
        scratch.append(vmem(2, 2, 2 * height, below))
        for shape in ((1, 2), (2, 1)):
            scratch += [
                vmem(*shape, 2 * height, half),
                vmem(2, *shape, 2 * height, half),
                vmem(2, 2 * height, half),
            ]
        scratch += [vmem(height, half), vmem(height, half)]
        shapes = out(height, below)
    else:
        blocks = below // BLOCK + 1
        shapes = [out(blocks, BLOCK, width)]
        if level:
            shapes.append(out(blocks, BLOCK, depth))
        shapes += [out(height, order) for height in heights]
    operands = operands + panels
    specs = [pl.BlockSpec(memory_space=pltpu.VMEM)] * len(operands)
    if level:
        specs[0] = pl.BlockSpec(memory_space=pltpu.SMEM)
    return pl.pallas_call(
        functools.partial(front_kernel, level, row_count, front, order),
        out_shape=shapes,
        in_specs=specs,
        scratch_shapes=scratch,
        name=f"front{level}",
        compiler_params=pltpu.CompilerParams(
            vmem_limit_bytes=60 * 2**20, collective_id=level, has_side_effects=True
        ),
    )(*operands)


def body(panel0, panel1, panel2, panel3, maps1, maps2, maps3):
    block_maps = (maps1, maps2, maps3)
    row_count = lax.axis_size("row")
    leaf = lax.axis_index("leaf")
    order = panel0.shape[1]
    front = panel0.shape[0] * row_count
    parents = front // BLOCK
    children = (front - order) // BLOCK
    operands = [panel0]
    waiting = [[panel1], [panel2, panel3], [], []]
    panels = []
    for level in range(LEVELS):
        outs = front_step(level, row_count, front, order, operands, waiting[level])
        if level == LEVELS - 1:
            return outs
        blocks = lax.dynamic_index_in_dim(block_maps[level], leaf // 2**level, 0, keepdims=False)
        hit = blocks[None, :] == jnp.arange(parents, dtype=jnp.int32)[:, None]
        back = jnp.min(
            jnp.where(hit, jnp.arange(children, dtype=jnp.int32)[None, :], children), axis=1
        )
        data = outs[: 2 if level else 1]
        panels += outs[len(data) :]
        operands = [back, panels[level], *data]


def solution(mesh):
    rows = P(("leaf", "row"), None)
    return jax.shard_map(
        body,
        mesh=mesh,
        in_specs=(rows, rows, rows, rows, P(), P(), P()),
        out_specs=rows,
        check_vma=False,
    )
```

```python
import functools
import math

import jax
import jax.numpy as jnp
from jax import lax
from jax.experimental import pallas as pl
from jax.experimental.pallas import tpu as pltpu
from jax.sharding import PartitionSpec as P

BLOCK = 128
SUB = 8
LEVELS = 4
CONTRACT_LAST = (((1,), (1,)), ((), ()))
CONTRACT_FIRST = (((1,), (0,)), ((), ()))


def halves(value):
    high = value.astype(jnp.bfloat16)
    low = (value - high.astype(jnp.float32)).astype(jnp.bfloat16)
    return high, low


def dot_split(left, right):
    left_high, left_low = left
    right_high, right_low = right

    def one(a, b):
        return lax.dot_general(a, b, CONTRACT_LAST, preferred_element_type=jnp.float32)

    return one(left_high, right_high) + (one(left_high, right_low) + one(left_low, right_high))


def dot_nt(left, right):
    return dot_split(halves(left), halves(right))


def spread(value, rows, columns):
    return jnp.broadcast_to(value, (rows, columns))


def diagonal_inverse(block, nothing, pause):
    count = BLOCK // SUB
    rows = [block[v * SUB : (v + 1) * SUB] for v in range(count)]
    lane = lax.broadcasted_iota(jnp.int32, (SUB, BLOCK), 1)
    sub = lax.broadcasted_iota(jnp.int32, (SUB, BLOCK), 0)
    for b in range(count):
        if b == count // 2:
            pause()
        base = b * SUB
        inside = (lane >= base) & (lane < base + SUB)
        own = rows[b]
        columns = [
            spread(own[:, base + j : base + j + 1], SUB, BLOCK) + nothing for j in range(SUB)
        ]
        a = [
            [spread(columns[j][i : i + 1], SUB, BLOCK) for j in range(i + 1)] for i in range(SUB)
        ]
        inverse = []
        ratio = [[None] * SUB for _ in range(SUB)]
        for i in range(SUB):
            inverse.append(1.0 / a[i][i])
            for j in range(i + 1, SUB):
                ratio[j][i] = a[j][i] * inverse[i]
            for j in range(i + 1, SUB):
                for k in range(i + 1, j + 1):
                    a[j][k] = a[j][k] - ratio[j][i] * a[k][i]
        cleared = jnp.where(inside, 0.0, own)
        pivots = []
        for j in range(SUB):
            row = spread(cleared[j : j + 1], SUB, BLOCK)
            row = jnp.where(lane == base + j, 1.0, row)
            for i in range(j):
                row = row - ratio[j][i] * pivots[i]
            pivots.append(row)
        for v in range(b + 1, count):
            old = rows[v]
            new = jnp.where(inside, 0.0, old)
            factors = []
            for j in range(SUB):
                column = spread(old[:, base + j : base + j + 1], SUB, BLOCK)
                for i in range(j):
                    column = column - factors[i] * a[j][i]
                factors.append(column * inverse[j])
            for j in range(SUB):
                new = new - factors[j] * pivots[j]
            rows[v] = new
        final = jnp.zeros((SUB, BLOCK), jnp.float32)
        scale = jnp.ones((SUB, BLOCK), jnp.float32)
        for j in range(SUB):
            final = jnp.where(sub == j, pivots[j], final)
            scale = jnp.where(sub == j, a[j][j], scale)
        rows[b] = jnp.where(lane <= sub + base, final / jnp.sqrt(scale), 0.0)
    return jnp.concatenate(rows, axis=0)


def neighbours(level):
    leaf = lax.axis_index("leaf")
    row = lax.axis_index("row")
    partners = []
    for bit in range(level):
        flag = leaf // 2**bit % 2
        partners.append({"leaf": leaf + (1 - 2 * flag) * 2**bit, "row": row})
    count = lax.axis_size("row")
    sibling = row + 1 - 2 * (row % 2)
    forward = [lax.rem(row + 2 * d, count) for d in range(1, count // 2)]
    backward = [lax.rem(row + count - 2 * d, count) for d in range(1, count // 2)]
    across = [{"leaf": leaf, "row": other} for other in forward]
    return partners, {"leaf": leaf, "row": sibling}, across, backward


def remote(source, target, sends, receives, slot, device):
    return pltpu.make_async_remote_copy(
        src_ref=source,
        dst_ref=target,
        send_sem=sends.at[slot],
        recv_sem=receives.at[slot],
        device_id=device,
        device_id_type=pl.DeviceIdType.MESH,
    )


class Gather:
    def __init__(self, buffer, place, sends, receives, slot, near, source=None):
        _, sibling, across, origins = near
        own = buffer.at[place(lax.axis_index("row"))]
        if source is None:
            source = own
        self.direct = remote(source, own, sends, receives, slot, sibling)
        self.far = []
        self.relay = []
        for n, (device, origin) in enumerate(zip(across, origins)):
            self.far.append(remote(source, own, sends, receives, slot + 1 + 2 * n, device))
            passed = buffer.at[place(origin)]
            self.relay.append(remote(passed, passed, sends, receives, slot + 2 + 2 * n, sibling))

    def start(self):
        for copy in self.far:
            copy.start()
        self.direct.start()

    def pass_on(self):
        for copy, relay in zip(self.far, self.relay):
            copy.wait_recv()
            relay.start()

    def finish(self):
        self.direct.wait_recv()
        for relay in self.relay:
            relay.wait_recv()
        for copy in [self.direct] + self.far + self.relay:
            copy.wait_send()


def rows_at(size, base=0):
    def place(row):
        return pl.ds(pl.multiple_of(row * size + base, 8), size)

    return place


def column_tiles(order):
    count = order // BLOCK
    return [(i, j) for j in range(count) for i in range(j, count)]


def pivot_chunks(order):
    count = order // BLOCK
    return [(0, 1), (1, count), (count, 2 * count - 1), (2 * count - 1, len(column_tiles(order)))]


def dot_split_nn(left, right):
    left_high, left_low = left
    right_high, right_low = right

    def one(a, b):
        return lax.dot_general(a, b, CONTRACT_FIRST, preferred_element_type=jnp.float32)

    return one(left_high, right_high) + (one(left_high, right_low) + one(left_low, right_high))


def entry_barrier(near):
    partners, sibling, across, _ = near
    barrier = pltpu.get_barrier_semaphore()
    peers = partners + [sibling] + across
    for peer in peers:
        pl.semaphore_signal(barrier, inc=1, device_id=peer, device_id_type=pl.DeviceIdType.MESH)
    return functools.partial(pl.semaphore_wait, barrier, len(peers))


def bit_reversed(index, bits):
    return sum((index >> b & 1) << (bits - 1 - b) for b in range(bits))


def rows_at_scaled(stride, base, size):
    def place(row):
        return pl.ds(pl.multiple_of(row * stride + base, 8), size)

    return place


class Links:
    def __init__(self, near, sends, receives):
        self.near = near
        self.sends = sends
        self.receives = receives
        self.used = 0

    def copy(self, source, target, device):
        slot = self.used
        self.used += 1
        return remote(source, target, self.sends, self.receives, slot, device)

    def gather(self, buffer, place, source=None):
        slot = self.used
        self.used += 1 + 2 * len(self.near[2])
        return Gather(buffer, place, self.sends, self.receives, slot, self.near, source)


def gather_task(move):
    return [move.start, move.pass_on, move.finish]


def sum_task(links, bits, share, span, inbox, sums, target, place):
    row = lax.axis_index("row")
    partners = links.near[0]
    moves = []
    for k, bit in enumerate(bits):
        source = share.at[span] if k == 0 else sums.at[k - 1, span]
        moves.append(links.copy(source, inbox.at[k, span], partners[bit]))
    spread = links.gather(target, place)

    def advance(k):
        moves[k].wait()
        total = (share[span] if k == 0 else sums[k - 1, span]) + inbox[k, span]
        if k + 1 < len(bits):
            sums[k, span] = total
            moves[k + 1].start()
        else:
            target[place(row)] = total
            spread.start()

    steps = [functools.partial(advance, k) for k in range(len(bits))]
    return [moves[0].start] + steps + [spread.pass_on, spread.finish]


def scatter_task(links, bits, share, start, height, inbox, sums, target, stride):
    row = lax.axis_index("row")
    leaf = lax.axis_index("leaf")
    partners = links.near[0]
    flags = [leaf // 2**bit % 2 for bit in bits]
    heights = [height // 2 ** (k + 1) for k in range(len(bits))]
    moves = []
    for k, bit in enumerate(bits):
        size = heights[k]
        other = pl.multiple_of((1 - flags[k]) * size, 8)
        if k == 0:
            source = share.at[pl.ds(start + other, size)]
        else:
            source = sums.at[k - 1, pl.ds(other, size)]
        moves.append(links.copy(source, inbox.at[k, pl.ds(0, size)], partners[bit]))
    regions = []
    origin = row * stride + start
    for flag, size in zip(flags, heights):
        origin = origin + flag * size
        regions.append(pl.ds(pl.multiple_of(origin, 8), size))
    returns = []
    for region, bit in reversed(list(zip(regions, bits))):
        returns.append(links.copy(target.at[region], target.at[region], partners[bit]))
    spread = links.gather(target, rows_at_scaled(stride, start, height))

    def reduce(k):
        size = heights[k]
        moves[k].wait()
        keep = pl.multiple_of(flags[k] * size, 8)
        mine = share[pl.ds(start + keep, size)] if k == 0 else sums[k - 1, pl.ds(keep, size)]
        total = mine + inbox[k, :size]
        if k + 1 < len(bits):
            sums[k, :size] = total
            moves[k + 1].start()
        else:
            target[regions[-1]] = total
            returns[0].start()

    def widen(k):
        returns[k].wait()
        if k + 1 < len(bits):
            returns[k + 1].start()
        else:
            spread.start()

    down = [functools.partial(reduce, k) for k in range(len(bits))]
    up = [functools.partial(widen, k) for k in range(len(bits))]
    return [moves[0].start] + down + up + [spread.pass_on, spread.finish]


def extra_task(links, bits, extra, columns, inbox, middle, final_in, result):
    leaf = lax.axis_index("leaf")
    partners = links.near[0]
    flags = [leaf // 2**bit % 2 for bit in range(LEVELS - 1)]
    size = result.shape[0]
    near, far = bits[0], bits[1]

    def pick(axis, flag):
        return (pl.ds(flag, 1), pl.ds(0, 2)) if axis == 0 else (pl.ds(0, 2), pl.ds(flag, 1))

    def inner(flag):
        return (pl.ds(0, 1), pl.ds(flag, 1)) if near == 0 else (pl.ds(flag, 1), pl.ds(0, 1))

    deep = LEVELS - 2
    half = lambda flag: pl.ds(pl.multiple_of(flag * size, 8), size)
    whole = pl.ds(0, 2 * size)
    give = extra.at[(*pick(near, 1 - flags[near]), whole, columns)]
    moves = [links.copy(give, inbox, partners[near])]
    moves.append(links.copy(middle.at[0].at[inner(1 - flags[far])], middle.at[1].at[(pl.ds(0, 1), pl.ds(0, 1))], partners[far]))
    moves.append(links.copy(final_in.at[0, half(1 - flags[deep])], final_in.at[1, pl.ds(0, size)], partners[deep]))

    def one():
        moves[0].wait()
        middle[0] = extra[(*pick(near, flags[near]), whole, columns)] + inbox[...]
        moves[1].start()

    def two():
        moves[1].wait()
        kept = middle[(0, *inner(flags[far]))] + middle[1, :1, :1]
        final_in[0] = kept.reshape(kept.shape[2:])
        moves[2].start()

    def three():
        moves[2].wait()
        result[...] = final_in[0, half(flags[deep])] + final_in[1, :size]

    return [moves[0].start, one, two, three]


def factor(diagonal, column, lower, inverse, spare, hook):
    order = lower.shape[1]
    tiles = order // BLOCK
    product, cross, block, zeros = spare
    row_ids = lax.broadcasted_iota(jnp.int32, (order, BLOCK), 0)

    def store(target, where, value):
        high, low = halves(value)
        target[(0, *where)] = high
        target[(1, *where)] = low

    def step(j, carry):
        hook(j, 0)
        start = pl.multiple_of(j * BLOCK, BLOCK)
        span = pl.ds(start, BLOCK)
        mine = lower[0, span], lower[1, span]
        product[...] = dot_split((lower[0], lower[1]), mine)
        cross[...] = dot_split_nn(mine, (inverse[0], inverse[1]))
        block[...] = diagonal_inverse(
            diagonal(j) - dot_split(mine, mine), zeros[...], functools.partial(hook, j, 1)
        )
        hook(j, 2)
        own = halves(block[...])
        below = jnp.where(row_ids >= start + BLOCK, column(j) - product[...], 0.0)
        store(lower, (slice(None), span), dot_split(halves(below), own))
        store(inverse, (span, slice(None)), -dot_split_nn(own, halves(cross[...])))
        inverse[0, span, span] = own[0]
        inverse[1, span, span] = own[1]
        return carry

    lax.fori_loop(0, tiles, step, 0)


def front_kernel(level, row_count, front, order, *refs):
    last = level == LEVELS - 1
    first = level == 0
    group = 2**level
    below = front - order
    count = order // BLOCK
    size = BLOCK // row_count
    refs = list(refs)
    take = lambda: refs.pop(0)
    row = lax.axis_index("row")
    member = lax.axis_index("leaf") % group
    old = kept = None
    if first:
        panel, *panels = take(), take()
    else:
        back, next_panel, fresh = take(), take(), take()
        old = take() if level > 1 else None
        panels = [take() for _ in range(LEVELS - 2)] if level == 1 else []
    result = take()
    if not first and not last:
        kept = take()
    joined = [take() for _ in panels]
    lower, inverse, product, cross, block, zeros = [take() for _ in range(6)]
    columns, sends, receives = [take() for _ in range(3)]
    held = [take() for _ in panels]
    near = neighbours(level)
    links = Links(near, sends, receives)
    arrived = entry_barrier(near)
    lower[...] = jnp.zeros_like(lower)
    inverse[...] = jnp.zeros_like(inverse)
    zeros[...] = jnp.zeros_like(zeros)
    panel_tasks = []
    for part, buffer in zip(panels, held):
        height = part.shape[0]
        panel_tasks.append(gather_task(links.gather(buffer, rows_at(height), part)))
        buffer[rows_at(height)(row)] = part[...]
    if first:
        arrived()
        gathered = take()
        chunk = panel.shape[0]

        def piece(base, height, left, width):
            def place(index):
                return rows_at_scaled(chunk, base, height)(index), pl.ds(left, width)

            source = panel.at[pl.ds(base, height), pl.ds(left, width)]
            return gather_task(links.gather(gathered, place, source))

        step = math.gcd(chunk, BLOCK)
        strips = [piece(base, step, 0, BLOCK) for base in range(0, chunk, step)]
        strips += [piece(0, chunk, left, BLOCK) for left in range(BLOCK, order, BLOCK)]
        for strip in strips:
            strip[0]()
        own = pl.ds(pl.multiple_of(row * chunk, 8), chunk)
        gathered[own] = panel[...]
        panel_tasks[0][0]()
        lead = chunk // step
        early = BLOCK // step
        for stage in (1, 2):
            for strip in strips[:early]:
                strip[stage]()
        rest = strips[early:lead]
        plan = {(0, 1): [s[1] for s in rest], (0, 2): [s[2] for s in rest]}
        for n, strip in enumerate(strips[lead:]):
            plan[n, 2] = plan.get((n, 2), []) + [strip[1]]
            plan[n + 1, 0] = [strip[2]]
        plan[count - 1, 2] = [panel_tasks[0][1]]
        after = []
        finally_ = panel_tasks[0][2:]

        def diagonal(j):
            span = pl.ds(pl.multiple_of(j * BLOCK, BLOCK), BLOCK)
            return gathered[span, span]

        def column(j):
            return gathered[:order, pl.ds(pl.multiple_of(j * BLOCK, BLOCK), BLOCK)]

    else:
        packed, pivot_share, pivot_sum, pivot_in = [take() for _ in range(4)]
        below_share, below_sum, below_in, placed, whole_panel = [take() for _ in range(5)]
        tasks = []
        turns = [list(range(level)), list(range(level))]
        if level > 1:
            turns[1][0], turns[1][1] = 1, 0
        for n, (begin, end) in enumerate(pivot_chunks(order)):

            def place(index, begin=begin, end=end):
                return pl.ds(begin, end - begin), pl.ds(pl.multiple_of(index * size, 8), size)

            bits = turns[n % 2] if n else turns[0]
            span = pl.ds(begin, end - begin)
            tasks.append(
                sum_task(links, bits, pivot_share, span, pivot_in, pivot_sum, packed, place)
            )
        share = below_share.shape[0]
        parts = 2 if last else 4
        height = share // parts
        for n in range(parts):
            if last:
                tasks.append(
                    scatter_task(
                        links, turns[n], below_share, n * height, height, below_in.at[n],
                        below_sum.at[n], columns, share,
                    )
                )
            else:
                tasks.append(
                    sum_task(
                        links, turns[n % 2], below_share, pl.ds(n * height, height), below_in,
                        below_sum, columns, rows_at_scaled(share, n * height, height),
                    )
                )
        a, b, c, d, e, f, *more = tasks
        both = lambda k: [e[k], f[k]]

        def fetch(i):
            target = slice(i * BLOCK, (i + 1) * BLOCK)
            depth = 0 if old is None else old.shape[2]
            if depth:
                placed[target, :depth] = old[back[i]]
            placed[target, depth:] = fresh[back[i]]

        whole_panel[...] = jnp.zeros_like(whole_panel)
        held_rows = next_panel.shape[0]
        whole_panel[pl.ds(pl.multiple_of(member * held_rows, 8), held_rows)] = next_panel[...]
        for i in range(front // BLOCK):
            fetch(i)
        pivots = halves(placed[:order])
        mine = [pl.ds(pl.multiple_of(i * BLOCK + row * size, 8), size) for i in range(count)]
        own = halves(jnp.concatenate([placed[span] for span in mine], axis=0))
        part = dot_split(own, pivots)
        for t, (i, j) in enumerate(column_tiles(order)):
            along = slice(j * BLOCK, (j + 1) * BLOCK)
            pivot_share[t] = whole_panel[mine[i], along] - part[i * size : (i + 1) * size, along]
        arrived()
        for task in (a, b, c, d):
            task[0]()
        spot = rows_at_scaled(share, order, share)(row)
        below_share[...] = whole_panel[spot] - dot_split(halves(placed[spot]), pivots)
        for task in [e, f] + more:
            task[0]()

        def keep():
            kept[: below // BLOCK] = placed[order:].reshape(below // BLOCK, *kept.shape[1:])
            kept[below // BLOCK] = jnp.zeros(kept.shape[1:], jnp.float32)

        finally_ = []
        if level == 1:
            g, h = more
            pre = [a[1], b[1], a[2], c[1], d[1]] + [t[0] for t in panel_tasks] + [keep, b[2], a[3]]
            plan = {
                (0, 1): [c[2], d[2], e[1]],
                (0, 2): [b[3]],
                (1, 0): [c[3], f[1]],
                (1, 1): [d[3], g[1]],
                (1, 2): [h[1], e[2]],
                (2, 1): [f[2], e[3]] + [t[1] for t in panel_tasks],
                (2, 2): [g[2]],
                (3, 0): [f[3]],
                (3, 1): [h[2], g[3]],
            }
            after = [h[3]]
            finally_ = [t[2] for t in panel_tasks]
        elif level == 2:
            g, h = more
            pre = [a[1], b[1], c[1], d[1], keep, a[2], b[2], c[2], d[2], e[1], f[1]]
            pre += [a[3], b[3], a[4]]
            plan = {
                (0, 1): [c[3], d[3], g[1], h[1]],
                (0, 2): [b[4]],
                (1, 0): [c[4], e[2], f[2]],
                (1, 1): [d[4]],
                (1, 2): [g[2], h[2], e[3]],
                (2, 1): [f[3], e[4]],
                (3, 0): [g[3]],
                (3, 1): [f[4], h[3]],
                (3, 2): [g[4]],
            }
            after = [h[4]]
        else:
            extra, inbox0, middle0, final0, inbox1, middle1, final1, sums0, sums1 = [
                take() for _ in range(9)
            ]
            half = below // 2
            x = extra_task(links, (0, 1), extra, pl.ds(0, half), inbox0, middle0, final0, sums0)
            y = extra_task(links, (1, 0), extra, pl.ds(half, half), inbox1, middle1, final1, sums1)

            def begin_extra():
                height = result.shape[0]
                rows = [None] * group
                for index in range(group):
                    start = pl.multiple_of(order + (index * row_count + row) * height, 8)
                    rows[bit_reversed(index, LEVELS - 1)] = placed[pl.ds(start, height)]
                part = halves(jnp.concatenate(rows, axis=0))
                for left, task in ((0, x), (half, y)):
                    other = halves(placed[order + left : order + left + half])
                    value = -dot_split(part, other)
                    extra[..., left : left + half] = value.reshape(*extra.shape[:3], half)
                    task[0]()

            pre = [a[1], b[1], a[2], b[2], c[1], d[1]] + both(1) + [c[2], d[2], begin_extra]
            pre += [a[3], b[3]] + both(2) + [a[4], c[3], d[3], b[4], a[5]]
            plan = {
                (0, 1): both(3) + [c[4], d[4]],
                (0, 2): [b[5]],
                (1, 0): [c[5]] + both(4),
                (1, 1): both(5),
                (1, 2): both(6),
                (2, 0): [d[5], x[1], y[1]],
                (2, 2): [x[2], y[2]],
                (3, 1): [e[7]],
                (3, 2): [e[8]],
            }
            after = [x[3], y[3], f[7], f[8]]
        for action in pre:
            action()

        def diagonal(j):
            return packed[j * count - j * (j - 1) // 2]

        def column(j):
            start = j * count - j * (j - 1) // 2 - j
            return packed[pl.ds(start, count)].reshape(order, BLOCK)

    def hook(j, slot):
        for (when, which), actions in plan.items():
            if which == slot:

                @pl.when(j == when)
                def _():
                    for action in actions:
                        action()

    factor(diagonal, column, lower, inverse, (product, cross, block, zeros), hook)
    for action in after:
        action()
    if last:
        height = result.shape[0]
        position = member * row_count + row
        own = columns[pl.ds(pl.multiple_of(position * height, 8), height)]
        whole = inverse[0], inverse[1]
        weight = dot_split_nn(halves(dot_split(halves(own), whole)), whole)
        rest = dot_nt(weight, columns[...])
        result[:, :half] = sums0[...] - rest[:, :half]
        result[:, half:] = sums1[...] - rest[:, half:]
        return
    width = order // group
    blocks = below // BLOCK
    if first:
        for left in range(0, order, 2 * BLOCK):
            right = min(left + 2 * BLOCK, order)
            part = inverse[0, left:right, :right], inverse[1, left:right, :right]
            value = dot_split(halves(gathered[order:, :right]), part)
            result[:blocks, :, left:right] = value.reshape(blocks, BLOCK, right - left)
    else:
        span = pl.ds(pl.multiple_of(member * width, BLOCK), width)
        value = dot_split(halves(columns[...]), (inverse[0, span], inverse[1, span]))
        result[:blocks] = value.reshape(blocks, BLOCK, width)
    result[blocks] = jnp.zeros((BLOCK, width), jnp.float32)
    for action in finally_:
        action()
    for buffer, target in zip(held, joined):
        target[...] = buffer[...]


def front_step(level, row_count, front, order, operands, panels):
    below = front - order
    width = order // 2**level
    tiles = len(column_tiles(order))
    float32 = jnp.float32

    def vmem(*shape, dtype=float32):
        return pltpu.VMEM(shape, dtype)

    def out(*shape):
        return jax.ShapeDtypeStruct(shape, float32)

    last = level == LEVELS - 1
    rest = below // row_count
    top = 2 ** (LEVELS - 1)
    copies = 8 * (row_count - 1) + 32
    scratch = [
        vmem(2, order, order, dtype=jnp.bfloat16),
        vmem(2, order, order, dtype=jnp.bfloat16),
        vmem(order, BLOCK),
        vmem(BLOCK, order),
        vmem(BLOCK, BLOCK),
        vmem(SUB, BLOCK),
        vmem(below if level else 8, order),
        pltpu.SemaphoreType.DMA((copies,)),
        pltpu.SemaphoreType.DMA((copies,)),
    ]
    heights = [row_count * panel.shape[0] for panel in panels]
    scratch += [vmem(height, order) for height in heights]
    depth = sum(order // 2**k for k in range(level))
    if level == 0:
        scratch.append(vmem(front, order))
    else:
        share = (tiles, BLOCK // row_count, BLOCK)
        scratch += [vmem(tiles, BLOCK, BLOCK), vmem(*share), vmem(level, *share), vmem(level, *share)]
        scratch.append(vmem(rest, order))
        if last:
            scratch += [vmem(2, level, rest // 4, order), vmem(2, level, rest // 4, order)]
        else:
            scratch += [vmem(level, rest, order), vmem(level, rest, order)]
        scratch += [vmem(front, depth), vmem(front, order)]
    if last:
        height = rest // top
        half = below // 2
        scratch.append(vmem(2, 2, 2 * height, below))
        for shape in ((1, 2), (2, 1)):
            scratch += [
                vmem(*shape, 2 * height, half),
                vmem(2, *shape, 2 * height, half),
                vmem(2, 2 * height, half),
            ]
        scratch += [vmem(height, half), vmem(height, half)]
        shapes = out(height, below)
    else:
        blocks = below // BLOCK + 1
        shapes = [out(blocks, BLOCK, width)]
        if level:
            shapes.append(out(blocks, BLOCK, depth))
        shapes += [out(height, order) for height in heights]
    operands = operands + panels
    specs = [pl.BlockSpec(memory_space=pltpu.VMEM)] * len(operands)
    if level:
        specs[0] = pl.BlockSpec(memory_space=pltpu.SMEM)
    return pl.pallas_call(
        functools.partial(front_kernel, level, row_count, front, order),
        out_shape=shapes,
        in_specs=specs,
        scratch_shapes=scratch,
        name=f"front{level}",
        compiler_params=pltpu.CompilerParams(
            vmem_limit_bytes=60 * 2**20, collective_id=level, has_side_effects=True
        ),
    )(*operands)


def body(panel0, panel1, panel2, panel3, maps1, maps2, maps3):
    block_maps = (maps1, maps2, maps3)
    row_count = lax.axis_size("row")
    leaf = lax.axis_index("leaf")
    order = panel0.shape[1]
    front = panel0.shape[0] * row_count
    parents = front // BLOCK
    children = (front - order) // BLOCK
    operands = [panel0]
    waiting = [[panel1], [panel2, panel3], [], []]
    panels = []
    for level in range(LEVELS):
        outs = front_step(level, row_count, front, order, operands, waiting[level])
        if level == LEVELS - 1:
            return outs
        blocks = lax.dynamic_index_in_dim(block_maps[level], leaf // 2**level, 0, keepdims=False)
        hit = blocks[None, :] == jnp.arange(parents, dtype=jnp.int32)[:, None]
        back = jnp.min(
            jnp.where(hit, jnp.arange(children, dtype=jnp.int32)[None, :], children), axis=1
        )
        data = outs[: 2 if level else 1]
        panels += outs[len(data) :]
        operands = [back, panels[level], *data]


def solution(mesh):
    rows = P(("leaf", "row"), None)
    return jax.shard_map(
        body,
        mesh=mesh,
        in_specs=(rows, rows, rows, rows, P(), P(), P()),
        out_specs=rows,
        check_vma=False,
    )
```
